256 devices in a mesh: shell: 2 (over core), row: 8 (over z), col: 16 (over x, y).
Axes of the slice: x: 4, y: 4, z: 8, core: 2. Of those that a mesh axis runs over, the one named last changes fastest.
Arguments:
- convergence: bfloat16 [2, 16384, 16384], P('shell', ('row', 'col')), may hold values from -6 to 6
- lens_weight: float32 [2], P('shell'), may hold values from 0.3 to 1
- rays_in: float32 [6, 1024, 16384], P(None, ('row', 'col')), may hold values from -6 to 6
Outputs:
- rays_out: float32 [2, 6, 1024, 16384], P('shell', None, ('row', 'col'))
The draws below stay inside these ranges and needn't reach their ends.
All inputs are finite; a program needn't handle non-finite values.
Results may differ from the reference program's by a relative error of at most 0.0003.
Values sent between devices are 32-bit elements; how exact they have to be, the bound alone decides.
A program may use at most 192 MiB of HBM per device.

```python
import math
import jax
import jax.numpy as jnp
from jax import lax

GRID = 16384
STRIDE = 16
SHELLS = 2
RAYS = 1024


def block_scale(stream_key, shape, pieces, least, top_value):
    gain, own = 1.0, jax.random.fold_in(stream_key, 6)
    for position, blocks in pieces:
        steps = jnp.exp(jax.random.uniform(jax.random.fold_in(own, position), (blocks,), jnp.float32, least / len(pieces), top_value / len(pieces)))
        gain = gain * jnp.repeat(steps, shape[position] // blocks).reshape([-1 if axis == position else 1 for axis in range(len(shape))])
    return gain


def gaussian(rng, shape, scale, limit, pieces=(), held_as=jnp.bfloat16):
    loudness = block_scale(rng, shape, pieces, -0.22, 0.18) if pieces else 1.0
    drawn = jax.random.normal(rng, shape, jnp.float32) * scale * loudness
    return jnp.minimum(jnp.maximum(drawn, -limit), limit).astype(held_as)


def setup_inputs(seed: int = 0) -> dict:
    arg_keys = jax.random.split(jax.random.key(seed), 4)
    convergence = gaussian(arg_keys[0], (SHELLS, GRID, GRID), 1.0, 6.0, ((0, 2), (1, 128)))
    lens_weight = jnp.clip(0.3 + 0.7 * jax.random.uniform(arg_keys[1], (SHELLS,), jnp.float32) ** block_scale(arg_keys[1], (SHELLS,), ((0, 2),), -0.2, 0.2), 0.3, 1.0)
    rays_in = gaussian(arg_keys[2], (6, RAYS, GRID), 1.0, 6.0, ((1, 128),), jnp.float32)
    return dict(convergence=convergence, lens_weight=lens_weight, rays_in=rays_in)


def shell_fields(kappa):
    length = kappa.shape[0]
    half = length // 2
    span = length // STRIDE
    spectrum = jnp.fft.rfft2(kappa.astype(jnp.float32))[:, :half]
    wave_cols = (2.0 * math.pi / length) * jnp.arange(half).astype(jnp.float32)

    def accumulate(total, alias):
        frequency = alias * span + jnp.arange(span, dtype=jnp.int32)
        signed = jnp.where(frequency < half, frequency, frequency - length).astype(jnp.float32)
        wave_rows = (2.0 * math.pi / length) * signed
        rows_part = wave_rows[:, None]
        cols_part = wave_cols[None, :]
        squared = rows_part * rows_part + cols_part * cols_part
        valid = (squared > 0.0) & (frequency != half)[:, None]
        scale = jnp.where(valid, -2.0 / jnp.where(valid, squared, 1.0), 0.0)
        piece = lax.dynamic_slice_in_dim(spectrum, alias * span, span, 0) * scale
        terms = jnp.stack([1j * rows_part * piece, 1j * cols_part * piece, -rows_part * rows_part * piece,
                           -cols_part * cols_part * piece, -rows_part * cols_part * piece])
        return total + terms, None

    total, _ = lax.scan(accumulate, jnp.zeros((5, span, half), spectrum.dtype), jnp.arange(STRIDE, dtype=jnp.int32))
    rows_done = jnp.fft.ifft(total, axis=1) / STRIDE
    return jnp.fft.irfft(rows_done, n=length, axis=2)


def advance(state, fields, weight):
    shift_rows = state[0] - weight * fields[0]
    shift_cols = state[1] - weight * fields[1]
    curve_rows, curve_cols, curve_mixed = fields[2], fields[3], fields[4]
    upper_left, upper_right, lower_left, lower_right = state[2], state[3], state[4], state[5]
    new_ul = upper_left - weight * (curve_rows * upper_left + curve_mixed * lower_left)
    new_ur = upper_right - weight * (curve_rows * upper_right + curve_mixed * lower_right)
    new_ll = lower_left - weight * (curve_mixed * upper_left + curve_cols * lower_left)
    new_lr = lower_right - weight * (curve_mixed * upper_right + curve_cols * lower_right)
    return jnp.stack([shift_rows, shift_cols, new_ul, new_ur, new_ll, new_lr])


def reference(convergence, lens_weight, rays_in):
    state = rays_in
    results = []
    for shell in range(SHELLS):
        fields = shell_fields(convergence[shell])
        state = advance(state, fields, lens_weight[shell])
        results.append(state)
    return jnp.stack(results)
```

```python
import math

import jax
import jax.numpy as jnp
import ml_dtypes
import numpy as np
from jax import lax
from jax.experimental import pallas as pl
from jax.experimental.pallas import tpu as pltpu
from jax.sharding import PartitionSpec as P


N = 16384
CHUNKS = 4
PER_CHUNK = 4 // CHUNKS
HELD = 16 * PER_CHUNK
ROWS = 32 * PER_CHUNK + 8
STEP = 2.0 * math.pi / N


def halves(table):
    table = np.asarray(table, np.float32)
    high = table.astype(ml_dtypes.bfloat16)
    low = (table - high.astype(np.float32)).astype(ml_dtypes.bfloat16)
    return high, low


def right_table(table):
    high, low = halves(table)
    return np.concatenate([high, high, low], axis=-2)


def left_table(table):
    high, low = halves(table)
    return np.concatenate([high, high, low], axis=-1)


def turns(first, second, length, sign):
    whole = np.outer(first, second) % length
    angle = sign * 2.0 * np.pi * whole / length
    return np.cos(angle), np.sin(angle)


def complex_right(first, second, length, sign):
    cosine, sine = turns(first, second, length, sign)
    return np.block([[cosine, sine], [-sine, cosine]])


def bins_of(chunk):
    return np.array([4 * y + PER_CHUNK * chunk + k for y in range(16) for k in range(PER_CHUNK)])


def forward_tables(chunk):
    t = bins_of(chunk)
    cosine, sine = turns(t, np.arange(64), 64, -1)
    high, low = halves(np.concatenate([cosine, sine], axis=0))
    first = np.concatenate([high, low], axis=1)
    twist = np.stack(turns(t, np.arange(256), N, -1)).astype(np.float32)
    second = right_table(complex_right(np.arange(256), np.arange(128), 256, -1))
    return first, twist, second


def row_tables():
    k = np.arange(128)
    grid = np.stack([right_table(complex_right(k, k + 128 * j, 1024, -1)) for j in range(8)])
    twist = np.zeros((8, 32, 128), np.float32)
    waves = np.zeros((8, 40, 128), np.float32)
    for j in range(8):
        base = k + 128 * j
        cosine, sine = turns(np.arange(16), base, N, -1)
        twist[j, 0::2], twist[j, 1::2] = cosine, sine
        for a in range(16):
            signed = base + 1024 * a - (N if a >= 8 else 0)
            wave = (2.0 * np.pi / N * signed).astype(np.float32)
            waves[j, a] = wave
            waves[j, 16 + a] = wave * wave
        waves[j, 32] = (base != 0).astype(np.float32)
    back = np.zeros((8, 16, 128), np.float32)
    for z in range(8):
        cosine, sine = turns(np.arange(8) - 128 * z, k, 1024, 1)
        back[z, 0::2], back[z, 1::2] = cosine * (-2.0 / N / N), sine * (-2.0 / N / N)
    cosine, sine = turns(k, k, 128, 1)
    left = left_table(np.block([[cosine, -sine], [sine, cosine]]))
    return grid, twist, waves, back, left


def final_tables():
    t = np.array([4 * y + k for k in range(4) for y in range(16)])
    first = right_table(complex_right(np.arange(128), np.arange(256), 256, 1))
    twist = np.stack(turns(t, np.arange(256), N, 1)).astype(np.float32)
    cosine, sine = turns(np.arange(64), t, 64, 1)
    second = left_table(np.concatenate([cosine, -sine], axis=1))
    bins = 64 * np.arange(128)[None, :] + t[:, None]
    wave = (2.0 * np.pi / N * bins).astype(np.float32)
    weight = np.where(bins == 0, 1.0, 2.0).astype(np.float32)
    scales = np.stack([weight, weight * wave, weight * wave * wave]).astype(np.float32)
    return first, twist, second, scales


def dot(left, right):
    return jnp.dot(left, right, preferred_element_type=jnp.float32)


def split(value):
    high = value.astype(jnp.bfloat16)
    low = (value - high.astype(jnp.float32)).astype(jnp.bfloat16)
    return high, low


def times(x, cosine, sine):
    return x[0] * cosine - x[1] * sine, x[0] * sine + x[1] * cosine


def plus(x, y):
    return x[0] + y[0], x[1] + y[1]


def minus(x, y):
    return x[0] - y[0], x[1] - y[1]


def quarter(x, sign):
    return (-x[1], x[0]) if sign > 0 else (x[1], -x[0])


def turned(x, eighths, sign):
    eighths %= 16
    if eighths == 0:
        return x
    if eighths == 4:
        return quarter(x, sign)
    if eighths == 2 or eighths == 6:
        root = math.sqrt(0.5)
        real, imaginary = x if eighths == 2 else quarter(x, sign)
        if sign > 0:
            return (real - imaginary) * root, (real + imaginary) * root
        return (real + imaginary) * root, (imaginary - real) * root
    angle = sign * 2.0 * math.pi * eighths / 16
    return times(x, math.cos(angle), math.sin(angle))


def four(x, sign):
    a, b = plus(x[0], x[2]), minus(x[0], x[2])
    c, d = plus(x[1], x[3]), quarter(minus(x[1], x[3]), sign)
    return [plus(a, c), plus(b, d), minus(a, c), minus(b, d)]


def sixteen(x, sign):
    inner = [four([x[4 * p + q] for p in range(4)], sign) for q in range(4)]
    out = [None] * 16
    for a in range(4):
        outer = four([turned(inner[q][a], q * a, sign) for q in range(4)], sign)
        for b in range(4):
            out[a + 4 * b] = outer[b]
    return out


def eight(x, sign):
    even, odd = four(x[0::2], sign), four(x[1::2], sign)
    odd = [turned(odd[i], 2 * i, sign) for i in range(4)]
    return [plus(even[i], odd[i]) for i in range(4)] + [minus(even[i], odd[i]) for i in range(4)]


def forward_kernel(k_ref, first_ref, twist_ref, second_ref, o_ref, l_ref):
    for r in range(8):
        row = k_ref[r]
        a = dot(first_ref[...], jnp.concatenate([row, row], axis=0))
        real, imaginary = times((a[:HELD], a[HELD:]), twist_ref[0], twist_ref[1])
        high, low = split(jnp.concatenate([real, imaginary], axis=1))
        l_ref[pl.ds(r * HELD, HELD), :] = jnp.concatenate([high, low, high], axis=1)
    out = dot(l_ref[...], second_ref[...])
    for part in range(2):
        piece = out[:, 128 * part : 128 * part + 128].reshape(8, HELD, 128)
        o_ref[:, part] = jnp.swapaxes(piece, 0, 1)


def whole(shape):
    return pl.BlockSpec(shape, lambda *_: (0,) * len(shape), pipeline_mode=pl.Buffered(1))


def forward(rows, chunk):
    first, twist, second = (jnp.asarray(x) for x in forward_tables(chunk))
    return pl.pallas_call(
        forward_kernel,
        grid=(16,),
        in_specs=[
            pl.BlockSpec((8, None, 64, 256), lambda v: (0, v, 0, 0)),
            whole(first.shape),
            whole(twist.shape),
            whole(second.shape),
        ],
        out_specs=pl.BlockSpec((HELD, 2, 8, 128), lambda v: (0, 0, v, 0)),
        out_shape=jax.ShapeDtypeStruct((HELD, 2, 128, 128), jnp.float32),
        scratch_shapes=[pltpu.VMEM((8 * HELD, 1536), jnp.bfloat16)],
        compiler_params=pltpu.CompilerParams(vmem_limit_bytes=40 << 20),
        cost_estimate=pl.CostEstimate(flops=2 * 128 * HELD * 2500 * 256, bytes_accessed=8 << 20, transcendentals=0),
        name="forward",
    )(rows, first, twist, second)


def filter_rows(z_ref, position, x_ref_twist, waves_ref, squares_ref, s_ref, q_ref):
    group, j = position // 8, position % 8
    for part in range(2):
        rows = pl.ds(pl.multiple_of(group * 16 + part * 8, 8), 8)
        square = squares_ref[rows, :]
        values = []
        for v in range(16):
            x = z_ref[v * 16 + part * 8 : v * 16 + part * 8 + 8, :128], z_ref[v * 16 + part * 8 : v * 16 + part * 8 + 8, 128:]
            if v:
                x = times(x, x_ref_twist[j, 2 * v : 2 * v + 1, :], x_ref_twist[j, 2 * v + 1 : 2 * v + 2, :])
            values.append(x)
        values = sixteen(values, -1)
        q_ref[j, 0, rows, :] = values[8][0] + jnp.where(square == 0.0, values[0][0], 0.0)
        q_ref[j, 1, rows, :] = values[8][1] + jnp.where(square == 0.0, values[0][1], 0.0)
        totals = None
        for a in range(16):
            wave = waves_ref[j, a : a + 1, :]
            below = waves_ref[j, 16 + a : 17 + a, :] + square
            if a == 0:
                scale = jnp.where(below > 0.0, 1.0 / jnp.where(below > 0.0, below, 1.0), 0.0)
            else:
                scale = 1.0 / below
            if a == 8:
                scale = scale * waves_ref[j, 32:33, :]
            real, imaginary = values[a][0] * scale, values[a][1] * scale
            terms = [real, imaginary, real * wave, imaginary * wave]
            totals = terms if totals is None else [p + t for p, t in zip(totals, terms)]
        for f in range(4):
            s_ref[f, j, rows, :] = totals[f]


def row_kernel(x_ref, squares_ref, grid_ref, twist_ref, waves_ref, back_ref, left_ref, o_ref, l_ref, z0_ref, z1_ref, s_ref, q_ref, g_ref, r_ref):
    k = pl.program_id(0)

    def arrange(v, _):
        rows = pl.ds(pl.multiple_of(v * 8, 8), 8)
        real = x_ref[:, 0, rows, :].reshape(128, 128)
        imaginary = x_ref[:, 1, rows, :].reshape(128, 128)
        high, low = split(jnp.concatenate([real.T, imaginary.T], axis=1))
        l_ref[:, v] = jnp.concatenate([high, low, high], axis=1).reshape(8, 16, 768)
        return 0

    lax.fori_loop(0, 16, arrange, 0)

    def multiply(position, z_ref):
        z_ref[...] = dot(l_ref[position // 8].reshape(256, 768), grid_ref[position % 8])

    def filtered(position, z_ref):
        filter_rows(z_ref, position, twist_ref, waves_ref, squares_ref, s_ref, q_ref)

    multiply(0, z0_ref)

    def pair(h, _):
        multiply(2 * h + 1, z1_ref)
        filtered(2 * h, z0_ref)
        multiply(jnp.minimum(2 * h + 2, 63), z0_ref)
        filtered(2 * h + 1, z1_ref)
        return 0

    lax.fori_loop(0, 32, pair, 0)

    def unfold(group, _):
        rows = pl.ds(pl.multiple_of(group * 16, 16), 16)
        for f in range(2):
            values = eight([(s_ref[2 * f, j, rows, :], s_ref[2 * f + 1, j, rows, :]) for j in range(8)], 1)
            for i in range(8):
                real, imaginary = times(values[i], back_ref[2 * i : 2 * i + 1, :], back_ref[2 * i + 1 : 2 * i + 2, :])
                high, low = split(jnp.concatenate([real, imaginary], axis=1))
                g_ref[8 * f + i, rows, :] = jnp.concatenate([high, low, high], axis=1)
        return 0

    lax.fori_loop(0, 8, unfold, 0)

    def outward(q, _):
        for e in range(4):
            result = lax.dot_general(left_ref[...], g_ref[4 * q + e], (((1,), (1,)), ((), ())), preferred_element_type=jnp.float32)
            r_ref[2 * e] = result[:128]
            r_ref[2 * e + 1] = result[128:]
        o_ref[:, pl.ds(pl.multiple_of(k * 32 + q * 8, 8), 8), :] = jnp.swapaxes(r_ref[...], 0, 1)
        return 0

    lax.fori_loop(0, 4, outward, 0)

    @pl.when(k == 0)
    def _():
        o_ref[:, 32 * PER_CHUNK :, :] = jnp.zeros((128, 8, 128), jnp.float32)

    for part in range(2):
        line = q_ref[0, part].T[0:1] * (1.0 / N / N)
        place = lax.broadcasted_iota(jnp.int32, (8, 128), 0) == 2 * k + part
        addend = jnp.where(place, jnp.broadcast_to(line, (8, 128)), 0.0)
        o_ref[:, 32 * PER_CHUNK :, :] += jnp.broadcast_to(addend[None], (128, 8, 128))


def row_stage(arrived, chunk, y, z):
    tables = [jnp.asarray(x) for x in row_tables()]
    tables[3] = lax.dynamic_index_in_dim(tables[3], z, 0, keepdims=False)
    t = 4 * y + PER_CHUNK * chunk + jnp.arange(PER_CHUNK, dtype=jnp.int32)
    wave = STEP * (64 * jnp.arange(128, dtype=jnp.int32)[None, :] + t[:, None]).astype(jnp.float32)
    squares = jnp.broadcast_to((wave * wave)[:, :, None], (PER_CHUNK, 128, 128))
    return pl.pallas_call(
        row_kernel,
        grid=(PER_CHUNK,),
        in_specs=[
            pl.BlockSpec((16, None, 2, 128, 128), lambda k: (0, k, 0, 0, 0)),
            pl.BlockSpec((None, 128, 128), lambda k: (k, 0, 0)),
        ]
        + [whole(x.shape) for x in tables],
        out_specs=whole((128, ROWS, 128)),
        out_shape=jax.ShapeDtypeStruct((128, ROWS, 128), jnp.float32),
        scratch_shapes=[
            pltpu.VMEM((8, 16, 16, 768), jnp.bfloat16),
            pltpu.VMEM((256, 256), jnp.float32),
            pltpu.VMEM((256, 256), jnp.float32),
            pltpu.VMEM((4, 8, 128, 128), jnp.float32),
            pltpu.VMEM((8, 2, 128, 128), jnp.float32),
            pltpu.VMEM((16, 128, 768), jnp.bfloat16),
            pltpu.VMEM((8, 128, 128), jnp.float32),
        ],
        compiler_params=pltpu.CompilerParams(vmem_limit_bytes=56 << 20),
        cost_estimate=pl.CostEstimate(flops=PER_CHUNK * 2 * 49152 * 65536, bytes_accessed=16 << 20, transcendentals=0),
        name="row_stage",
    )(arrived.reshape(16, PER_CHUNK, 2, 128, 128), squares, *tables)


def final_kernel(*refs):
    y_refs, (k_ref, first_ref, twist_ref, second_ref, scales_ref, o_ref, a_ref, b_ref, r_ref, f_ref) = refs[:CHUNKS], refs[CHUNKS:]
    for chunk in range(CHUNKS):
        for k in range(PER_CHUNK):
            place = 16 * (chunk * PER_CHUNK + k)
            for q in range(4):
                block = y_refs[chunk][:, 32 * k + 8 * q : 32 * k + 8 * q + 8, :]
                a_ref[8 * q : 8 * q + 8, place : place + 16, :] = jnp.swapaxes(block, 0, 1)
        block = jnp.swapaxes(y_refs[chunk][:, 32 * PER_CHUNK :, :], 0, 1)
        for k in range(PER_CHUNK):
            place = 16 * (chunk * PER_CHUNK + k)
            for part in range(2):
                a_ref[32 + part, place : place + 16, :] = block[2 * k + part]

    def synthesis(pairs):
        high, low = split(jnp.concatenate([jnp.concatenate(p, axis=1) for p in pairs], axis=0))
        out = dot(jnp.concatenate([high, low, high], axis=1), first_ref[...])
        results = []
        for f in range(len(pairs)):
            x = out[64 * f : 64 * f + 64, :256], out[64 * f : 64 * f + 64, 256:]
            high, low = split(jnp.concatenate(times(x, twist_ref[0], twist_ref[1]), axis=0))
            results.append(dot(second_ref[...], jnp.concatenate([high, low, high], axis=0)))
        return results

    weight = scales_ref[0]
    r_ref[...] = synthesis([(a_ref[32] * weight, a_ref[33] * weight)])[0]
    sign = (1 - 2 * (lax.broadcasted_iota(jnp.int32, (64, 256), 1) % 2)).astype(jnp.float32)

    def ray(i, _):
        base = a_ref[2 * i], a_ref[2 * i + 1]
        slope = a_ref[16 + 2 * i], a_ref[17 + 2 * i]
        one, wave, square = scales_ref[0], scales_ref[1], scales_ref[2]
        alpha_rows, alpha_cols, curve_cols, curve_mixed = synthesis(
            [
                (-slope[1] * one, slope[0] * one),
                (-base[1] * wave, base[0] * wave),
                (-base[0] * square, -base[1] * square),
                (-slope[0] * wave, -slope[1] * wave),
            ]
        )
        kappa = k_ref[i].astype(jnp.float32)
        edge = sign * (jnp.sum(kappa * sign) * (1.0 / N))
        curve_rows = 2.0 * (kappa - edge - r_ref[...]) - curve_cols
        for f, field in enumerate([alpha_rows, alpha_cols, curve_rows, curve_cols, curve_mixed]):
            f_ref[f, i] = field
        return 0

    lax.fori_loop(0, 8, ray, 0)
    for f in range(5):
        for g in range(8):
            block = jnp.swapaxes(f_ref[f, :, 8 * g : 8 * g + 8, :], 0, 1)
            for v in range(8):
                o_ref[f, :, (8 * g + v) * 256 : (8 * g + v) * 256 + 256] = block[v]


def final_stage(returned, rows):
    tables = [jnp.asarray(x) for x in final_tables()]
    return pl.pallas_call(
        final_kernel,
        grid=(1,),
        in_specs=[whole((16, ROWS, 128))] * CHUNKS
        + [pl.BlockSpec((8, None, 64, 256), lambda v: (0, 0, 0, 0))]
        + [whole(x.shape) for x in tables],
        out_specs=whole((5, 8, N)),
        out_shape=jax.ShapeDtypeStruct((5, 8, N), jnp.float32),
        scratch_shapes=[
            pltpu.VMEM((34, 64, 128), jnp.float32),
            pltpu.VMEM((8, 128), jnp.float32),
            pltpu.VMEM((64, 256), jnp.float32),
            pltpu.VMEM((5, 8, 64, 256), jnp.float32),
        ],
        compiler_params=pltpu.CompilerParams(vmem_limit_bytes=40 << 20),
        cost_estimate=pl.CostEstimate(flops=2 * 16384 * 65536, bytes_accessed=8 << 20, transcendentals=0),
        name="final_stage",
    )(*returned, rows, *tables)


def advance_kernel(w_ref, s_ref, f_ref, o_ref):
    w = w_ref[0]
    o_ref[0] = s_ref[0] - w * f_ref[0]
    o_ref[1] = s_ref[1] - w * f_ref[1]
    rows, cols, mixed = w * f_ref[2], w * f_ref[3], w * f_ref[4]
    upper_left, upper_right, lower_left, lower_right = s_ref[2], s_ref[3], s_ref[4], s_ref[5]
    o_ref[2] = upper_left - (rows * upper_left + mixed * lower_left)
    o_ref[3] = upper_right - (rows * upper_right + mixed * lower_right)
    o_ref[4] = lower_left - (mixed * upper_left + cols * lower_left)
    o_ref[5] = lower_right - (mixed * upper_right + cols * lower_right)


def advance(state, fields, weight):
    width = 2048
    return pl.pallas_call(
        advance_kernel,
        grid=(N // width,),
        in_specs=[
            pl.BlockSpec(memory_space=pltpu.SMEM),
            pl.BlockSpec((6, 8, width), lambda p: (0, 0, p)),
            pl.BlockSpec((5, 8, width), lambda p: (0, 0, p)),
        ],
        out_specs=pl.BlockSpec((6, 8, width), lambda p: (0, 0, p)),
        out_shape=jax.ShapeDtypeStruct((6, 8, N), jnp.float32),
        cost_estimate=pl.CostEstimate(flops=22 * 8 * N, bytes_accessed=17 * 8 * N * 4, transcendentals=0),
        name="advance",
    )(weight, state, fields)


def exchanged(value):
    return lax.all_to_all(value, "col", split_axis=0, concat_axis=0, tiled=True)


def body(convergence, lens_weight, rays_in):
    y, z = lax.axis_index("col"), lax.axis_index("row")
    rows = convergence.reshape(8, 16, 64, 256)
    sent, summed, returned = [], [], []
    for chunk in range(CHUNKS):
        sent.append(forward(rows, chunk))
    for chunk in range(CHUNKS):
        arrived = exchanged(sent[chunk])
        partial = row_stage(arrived, chunk, y, z)
        summed.append(lax.psum_scatter(partial, "row", scatter_dimension=0, tiled=True))
    for chunk in range(CHUNKS):
        returned.append(exchanged(summed[chunk]))
    fields = final_stage(returned, rows)
    state = advance(rays_in, fields, lens_weight)
    received = lax.ppermute(state, "shell", [(0, 1)])
    start = jnp.where(lax.axis_index("shell") == 1, received, rays_in)
    return advance(start, fields, lens_weight)[None]


def solution(mesh):
    in_specs = (P("shell", ("row", "col"), None), P("shell"), P(None, ("row", "col"), None))
    out_specs = P("shell", None, ("row", "col"), None)
    return jax.shard_map(body, mesh=mesh, in_specs=in_specs, out_specs=out_specs, check_vma=False)
```

```python
import math

import jax
import jax.numpy as jnp
import ml_dtypes
import numpy as np
from jax import lax
from jax.experimental import pallas as pl
from jax.experimental.pallas import tpu as pltpu
from jax.sharding import PartitionSpec as P


N = 16384
CHUNKS = 4
PER_CHUNK = 4 // CHUNKS
HELD = 16 * PER_CHUNK
ROWS = 32 * PER_CHUNK + 8
GROUP = 2
STEP = 2.0 * math.pi / N


def halves(table):
    table = np.asarray(table, np.float32)
    high = table.astype(ml_dtypes.bfloat16)
    low = (table - high.astype(np.float32)).astype(ml_dtypes.bfloat16)
    return high, low


def right_table(table):
    high, low = halves(table)
    return np.concatenate([high, high, low], axis=-2)


def left_table(table):
    high, low = halves(table)
    return np.concatenate([high, high, low], axis=-1)


def turns(first, second, length, sign):
    whole = np.outer(first, second) % length
    angle = sign * 2.0 * np.pi * whole / length
    return np.cos(angle), np.sin(angle)


def complex_right(first, second, length, sign):
    cosine, sine = turns(first, second, length, sign)
    return np.block([[cosine, sine], [-sine, cosine]])


def bins_of(chunk):
    return np.array([4 * y + PER_CHUNK * chunk + k for y in range(16) for k in range(PER_CHUNK)])


def forward_tables(chunk):
    t = bins_of(chunk)
    cosine, sine = turns(t, np.arange(64), 64, -1)
    high, low = halves(np.concatenate([cosine, sine], axis=0))
    first = np.concatenate([high, low], axis=1)
    twist = np.stack(turns(t, np.arange(256), N, -1)).astype(np.float32)
    second = right_table(complex_right(np.arange(256), np.arange(128), 256, -1))
    return first, twist, second


def row_tables():
    k = np.arange(128)
    grid = np.stack([right_table(complex_right(k, k + 128 * j, 1024, -1)) for j in range(8)])
    twist = np.zeros((8, 32, 128), np.float32)
    waves = np.zeros((8, 40, 128), np.float32)
    for j in range(8):
        base = k + 128 * j
        cosine, sine = turns(np.arange(16), base, N, -1)
        twist[j, 0::2], twist[j, 1::2] = cosine, sine
        for a in range(16):
            signed = base + 1024 * a - (N if a >= 8 else 0)
            wave = (2.0 * np.pi / N * signed).astype(np.float32)
            waves[j, a] = wave
            waves[j, 16 + a] = wave * wave
        waves[j, 32] = (base != 0).astype(np.float32)
    back = np.zeros((8, 16, 128), np.float32)
    for z in range(8):
        cosine, sine = turns(np.arange(8) - 128 * z, k, 1024, 1)
        back[z, 0::2], back[z, 1::2] = cosine * (-2.0 / N / N), sine * (-2.0 / N / N)
    cosine, sine = turns(k, k, 128, 1)
    left = left_table(np.block([[cosine, -sine], [sine, cosine]]))
    return grid, twist, waves, back, left


def final_tables():
    t = np.array([4 * y + k for k in range(4) for y in range(16)])
    first = right_table(complex_right(np.arange(128), np.arange(256), 256, 1))
    twist = np.stack(turns(t, np.arange(256), N, 1)).astype(np.float32)
    cosine, sine = turns(np.arange(64), t, 64, 1)
    second = left_table(np.concatenate([cosine, -sine], axis=1))
    bins = 64 * np.arange(128)[None, :] + t[:, None]
    wave = (2.0 * np.pi / N * bins).astype(np.float32)
    weight = np.where(bins == 0, 1.0, 2.0).astype(np.float32)
    scales = np.stack([weight, weight * wave, weight * wave * wave]).astype(np.float32)
    return first, twist, second, scales


def dot(left, right):
    return jnp.dot(left, right, preferred_element_type=jnp.float32)


def split(value):
    high = value.astype(jnp.bfloat16)
    low = (value - high.astype(jnp.float32)).astype(jnp.bfloat16)
    return high, low


def times(x, cosine, sine):
    return x[0] * cosine - x[1] * sine, x[0] * sine + x[1] * cosine


def plus(x, y):
    return x[0] + y[0], x[1] + y[1]


def minus(x, y):
    return x[0] - y[0], x[1] - y[1]


def quarter(x, sign):
    return (-x[1], x[0]) if sign > 0 else (x[1], -x[0])


def turned(x, eighths, sign):
    eighths %= 16
    if eighths == 0:
        return x
    if eighths == 4:
        return quarter(x, sign)
    if eighths == 2 or eighths == 6:
        root = math.sqrt(0.5)
        real, imaginary = x if eighths == 2 else quarter(x, sign)
        if sign > 0:
            return (real - imaginary) * root, (real + imaginary) * root
        return (real + imaginary) * root, (imaginary - real) * root
    angle = sign * 2.0 * math.pi * eighths / 16
    return times(x, math.cos(angle), math.sin(angle))


def four(x, sign):
    a, b = plus(x[0], x[2]), minus(x[0], x[2])
    c, d = plus(x[1], x[3]), quarter(minus(x[1], x[3]), sign)
    return [plus(a, c), plus(b, d), minus(a, c), minus(b, d)]


def sixteen(x, sign):
    inner = [four([x[4 * p + q] for p in range(4)], sign) for q in range(4)]
    out = [None] * 16
    for a in range(4):
        outer = four([turned(inner[q][a], q * a, sign) for q in range(4)], sign)
        for b in range(4):
            out[a + 4 * b] = outer[b]
    return out


def eight(x, sign):
    even, odd = four(x[0::2], sign), four(x[1::2], sign)
    odd = [turned(odd[i], 2 * i, sign) for i in range(4)]
    return [plus(even[i], odd[i]) for i in range(4)] + [minus(even[i], odd[i]) for i in range(4)]


def forward_kernel(k_ref, first_ref, twist_ref, second_ref, o_ref, l_ref):
    for r in range(8):
        row = k_ref[r]
        a = dot(first_ref[...], jnp.concatenate([row, row], axis=0))
        real, imaginary = times((a[:HELD], a[HELD:]), twist_ref[0], twist_ref[1])
        high, low = split(jnp.concatenate([real, imaginary], axis=1))
        l_ref[pl.ds(r * HELD, HELD), :] = jnp.concatenate([high, low, high], axis=1)
    out = dot(l_ref[...], second_ref[...])
    for part in range(2):
        piece = out[:, 128 * part : 128 * part + 128].reshape(8, HELD, 128)
        o_ref[:, part] = jnp.swapaxes(piece, 0, 1)


def whole(shape):
    return pl.BlockSpec(shape, lambda *_: (0,) * len(shape), pipeline_mode=pl.Buffered(1))


def forward(rows, chunk):
    first, twist, second = (jnp.asarray(x) for x in forward_tables(chunk))
    return pl.pallas_call(
        forward_kernel,
        grid=(16,),
        in_specs=[
            pl.BlockSpec((8, None, 64, 256), lambda v: (0, v, 0, 0)),
            whole(first.shape),
            whole(twist.shape),
            whole(second.shape),
        ],
        out_specs=pl.BlockSpec((HELD, 2, 8, 128), lambda v: (0, 0, v, 0)),
        out_shape=jax.ShapeDtypeStruct((HELD, 2, 128, 128), jnp.float32),
        scratch_shapes=[pltpu.VMEM((8 * HELD, 1536), jnp.bfloat16)],
        compiler_params=pltpu.CompilerParams(vmem_limit_bytes=40 << 20),
        cost_estimate=pl.CostEstimate(flops=2 * 128 * HELD * 2500 * 256, bytes_accessed=8 << 20, transcendentals=0),
        name="forward",
    )(rows, first, twist, second)


def filter_rows(z_ref, position, x_ref_twist, waves_ref, squares_ref, s_ref, q_ref):
    group, j = position // 8, position % 8
    for part in range(2):
        rows = pl.ds(pl.multiple_of(group * 16 + part * 8, 8), 8)
        square = squares_ref[rows, :]
        values = []
        for v in range(16):
            x = z_ref[v * 16 + part * 8 : v * 16 + part * 8 + 8, :128], z_ref[v * 16 + part * 8 : v * 16 + part * 8 + 8, 128:]
            if v:
                x = times(x, x_ref_twist[j, 2 * v : 2 * v + 1, :], x_ref_twist[j, 2 * v + 1 : 2 * v + 2, :])
            values.append(x)
        values = sixteen(values, -1)
        q_ref[j, 0, rows, :] = values[8][0] + jnp.where(square == 0.0, values[0][0], 0.0)
        q_ref[j, 1, rows, :] = values[8][1] + jnp.where(square == 0.0, values[0][1], 0.0)
        totals = None
        for a in range(16):
            wave = waves_ref[j, a : a + 1, :]
            below = waves_ref[j, 16 + a : 17 + a, :] + square
            if a == 0:
                scale = jnp.where(below > 0.0, 1.0 / jnp.where(below > 0.0, below, 1.0), 0.0)
            else:
                scale = 1.0 / below
            if a == 8:
                scale = scale * waves_ref[j, 32:33, :]
            real, imaginary = values[a][0] * scale, values[a][1] * scale
            terms = [real, imaginary, real * wave, imaginary * wave]
            totals = terms if totals is None else [p + t for p, t in zip(totals, terms)]
        for f in range(4):
            s_ref[f, j, rows, :] = totals[f]


def row_kernel(x_ref, squares_ref, grid_ref, twist_ref, waves_ref, back_ref, left_ref, *rest):
    o_ref, l_ref, z0_ref, z1_ref, s_ref, q_ref, g_ref, r_ref = rest[-8:]
    k = pl.program_id(0)

    def arrange(v, _):
        rows = pl.ds(pl.multiple_of(v * 8, 8), 8)
        real = x_ref[:, 0, rows, :].reshape(128, 128)
        imaginary = x_ref[:, 1, rows, :].reshape(128, 128)
        high, low = split(jnp.concatenate([real.T, imaginary.T], axis=1))
        l_ref[:, v] = jnp.concatenate([high, low, high], axis=1).reshape(8, 16, 768)
        return 0

    lax.fori_loop(0, 16, arrange, 0)

    def multiply(position, z_ref):
        z_ref[...] = dot(l_ref[position // 8].reshape(256, 768), grid_ref[position % 8])

    def filtered(position, z_ref):
        filter_rows(z_ref, position, twist_ref, waves_ref, squares_ref, s_ref, q_ref)

    multiply(0, z0_ref)

    def pair(h, _):
        multiply(2 * h + 1, z1_ref)
        filtered(2 * h, z0_ref)
        multiply(jnp.minimum(2 * h + 2, 63), z0_ref)
        filtered(2 * h + 1, z1_ref)
        return 0

    lax.fori_loop(0, 32, pair, 0)

    def unfold(group, _):
        rows = pl.ds(pl.multiple_of(group * 16, 16), 16)
        for f in range(2):
            values = eight([(s_ref[2 * f, j, rows, :], s_ref[2 * f + 1, j, rows, :]) for j in range(8)], 1)
            for i in range(8):
                real, imaginary = times(values[i], back_ref[2 * i : 2 * i + 1, :], back_ref[2 * i + 1 : 2 * i + 2, :])
                high, low = split(jnp.concatenate([real, imaginary], axis=1))
                g_ref[8 * f + i, rows, :] = jnp.concatenate([high, low, high], axis=1)
        return 0

    lax.fori_loop(0, 8, unfold, 0)

    def outward(q, _):
        for e in range(4):
            result = lax.dot_general(left_ref[...], g_ref[4 * q + e], (((1,), (1,)), ((), ())), preferred_element_type=jnp.float32)
            r_ref[2 * e] = result[:128]
            r_ref[2 * e + 1] = result[128:]
        o_ref[:, pl.ds(pl.multiple_of(k * 32 + q * 8, 8), 8), :] = jnp.swapaxes(r_ref[...], 0, 1)
        return 0

    lax.fori_loop(0, 4, outward, 0)

    @pl.when(k == 0)
    def _():
        o_ref[:, 32 * PER_CHUNK :, :] = jnp.zeros((128, 8, 128), jnp.float32)

    for part in range(2):
        line = q_ref[0, part].T[0:1] * (1.0 / N / N)
        place = lax.broadcasted_iota(jnp.int32, (8, 128), 0) == 2 * k + part
        addend = jnp.where(place, jnp.broadcast_to(line, (8, 128)), 0.0)
        o_ref[:, 32 * PER_CHUNK :, :] += jnp.broadcast_to(addend[None], (128, 8, 128))


def row_stage(arrived, chunk, y, z, previous):
    tables = [jnp.asarray(x) for x in row_tables()]
    held, section = [previous] if previous is not None else [], chunk % GROUP
    tables[3] = lax.dynamic_index_in_dim(tables[3], z, 0, keepdims=False)
    t = 4 * y + PER_CHUNK * chunk + jnp.arange(PER_CHUNK, dtype=jnp.int32)
    wave = STEP * (64 * jnp.arange(128, dtype=jnp.int32)[None, :] + t[:, None]).astype(jnp.float32)
    squares = jnp.broadcast_to((wave * wave)[:, :, None], (PER_CHUNK, 128, 128))
    return pl.pallas_call(
        row_kernel,
        grid=(PER_CHUNK,),
        in_specs=[
            pl.BlockSpec((16, None, 2, 128, 128), lambda k: (0, k, 0, 0, 0)),
            pl.BlockSpec((None, 128, 128), lambda k: (k, 0, 0)),
        ]
        + [whole(x.shape) for x in tables]
        + [pl.BlockSpec(memory_space=pl.ANY)] * len(held),
        out_specs=pl.BlockSpec((128, ROWS, 128), lambda k: (0, section, 0), pipeline_mode=pl.Buffered(1)),
        out_shape=jax.ShapeDtypeStruct((128, GROUP * ROWS, 128), jnp.float32),
        input_output_aliases={7: 0} if held else {},
        scratch_shapes=[
            pltpu.VMEM((8, 16, 16, 768), jnp.bfloat16),
            pltpu.VMEM((256, 256), jnp.float32),
            pltpu.VMEM((256, 256), jnp.float32),
            pltpu.VMEM((4, 8, 128, 128), jnp.float32),
            pltpu.VMEM((8, 2, 128, 128), jnp.float32),
            pltpu.VMEM((16, 128, 768), jnp.bfloat16),
            pltpu.VMEM((8, 128, 128), jnp.float32),
        ],
        compiler_params=pltpu.CompilerParams(vmem_limit_bytes=56 << 20),
        cost_estimate=pl.CostEstimate(flops=PER_CHUNK * 2 * 49152 * 65536, bytes_accessed=16 << 20, transcendentals=0),
        name="row_stage",
    )(arrived.reshape(16, PER_CHUNK, 2, 128, 128), squares, *tables, *held)


def final_kernel(*refs):
    count = CHUNKS // GROUP
    y_refs = [refs[c // GROUP].at[:, pl.ds(c % GROUP * ROWS, ROWS), :] for c in range(CHUNKS)]
    w_ref, state_ref, k_ref, first_ref, twist_ref, second_ref, scales_ref, o_ref, n_ref, a_ref, r_ref, f_ref = refs[count:]
    for chunk in range(CHUNKS):
        for k in range(PER_CHUNK):
            place = 16 * (chunk * PER_CHUNK + k)
            for q in range(4):
                block = y_refs[chunk][:, 32 * k + 8 * q : 32 * k + 8 * q + 8, :]
                a_ref[8 * q : 8 * q + 8, place : place + 16, :] = jnp.swapaxes(block, 0, 1)
        block = jnp.swapaxes(y_refs[chunk][:, 32 * PER_CHUNK :, :], 0, 1)
        for k in range(PER_CHUNK):
            place = 16 * (chunk * PER_CHUNK + k)
            for part in range(2):
                a_ref[32 + part, place : place + 16, :] = block[2 * k + part]

    def synthesis(pairs):
        high, low = split(jnp.concatenate([jnp.concatenate(p, axis=1) for p in pairs], axis=0))
        out = dot(jnp.concatenate([high, low, high], axis=1), first_ref[...])
        results = []
        for f in range(len(pairs)):
            x = out[64 * f : 64 * f + 64, :256], out[64 * f : 64 * f + 64, 256:]
            high, low = split(jnp.concatenate(times(x, twist_ref[0], twist_ref[1]), axis=0))
            results.append(dot(second_ref[...], jnp.concatenate([high, low, high], axis=0)))
        return results

    weight = scales_ref[0]
    r_ref[...] = synthesis([(a_ref[32] * weight, a_ref[33] * weight)])[0]
    sign = (1 - 2 * (lax.broadcasted_iota(jnp.int32, (64, 256), 1) % 2)).astype(jnp.float32)

    def ray(i, _):
        base = a_ref[2 * i], a_ref[2 * i + 1]
        slope = a_ref[16 + 2 * i], a_ref[17 + 2 * i]
        one, wave, square = scales_ref[0], scales_ref[1], scales_ref[2]
        alpha_rows, alpha_cols, curve_cols, curve_mixed = synthesis(
            [
                (-slope[1] * one, slope[0] * one),
                (-base[1] * wave, base[0] * wave),
                (-base[0] * square, -base[1] * square),
                (-slope[0] * wave, -slope[1] * wave),
            ]
        )
        kappa = k_ref[i].astype(jnp.float32)
        edge = sign * (jnp.sum(kappa * sign) * (1.0 / N))
        curve_rows = 2.0 * (kappa - edge - r_ref[...]) - curve_cols
        for f, field in enumerate([alpha_rows, alpha_cols, curve_rows, curve_cols, curve_mixed]):
            f_ref[f, i] = field
        return 0

    lax.fori_loop(0, 8, ray, 0)

    def emit(g, _):
        blocks = [jnp.swapaxes(f_ref[f, :, pl.ds(pl.multiple_of(8 * g, 8), 8), :], 0, 1) for f in range(5)]
        for v in range(8):
            place = pl.ds(pl.multiple_of((8 * g + v) * 256, 256), 256)
            fields = [block[v] for block in blocks]
            for f in range(5):
                o_ref[f, :, place] = fields[f]
            for e, value in enumerate(moved([state_ref[e, :, place] for e in range(6)], fields, w_ref[0])):
                n_ref[e, :, place] = value
        return 0

    lax.fori_loop(0, 8, emit, 0)


def moved(state, fields, w):
    rows, cols, mixed = w * fields[2], w * fields[3], w * fields[4]
    upper_left, upper_right, lower_left, lower_right = state[2:]
    return [
        state[0] - w * fields[0],
        state[1] - w * fields[1],
        upper_left - (rows * upper_left + mixed * lower_left),
        upper_right - (rows * upper_right + mixed * lower_right),
        lower_left - (mixed * upper_left + cols * lower_left),
        lower_right - (mixed * upper_right + cols * lower_right),
    ]


def final_stage(returned, rows, weight, state):
    tables = [jnp.asarray(x) for x in final_tables()]
    return pl.pallas_call(
        final_kernel,
        grid=(1,),
        in_specs=[whole((16, GROUP * ROWS, 128))] * (CHUNKS // GROUP)
        + [pl.BlockSpec(memory_space=pltpu.SMEM), whole((6, 8, N))]
        + [pl.BlockSpec((8, None, 64, 256), lambda v: (0, 0, 0, 0))]
        + [whole(x.shape) for x in tables],
        out_specs=[whole((5, 8, N)), whole((6, 8, N))],
        out_shape=[jax.ShapeDtypeStruct((5, 8, N), jnp.float32), jax.ShapeDtypeStruct((6, 8, N), jnp.float32)],
        scratch_shapes=[
            pltpu.VMEM((34, 64, 128), jnp.float32),
            pltpu.VMEM((64, 256), jnp.float32),
            pltpu.VMEM((5, 8, 64, 256), jnp.float32),
        ],
        compiler_params=pltpu.CompilerParams(vmem_limit_bytes=40 << 20),
        cost_estimate=pl.CostEstimate(flops=2 * 16384 * 65536, bytes_accessed=8 << 20, transcendentals=0),
        name="final_stage",
    )(*returned, weight, state, rows, *tables)


def advance_kernel(w_ref, second_ref, s_ref, f_ref, n_ref, o_ref):
    last = second_ref[0] == 1
    values = moved([s_ref[e] for e in range(6)], [f_ref[f] for f in range(5)], w_ref[0])
    for e in range(6):
        o_ref[e] = jnp.where(last, values[e], n_ref[e])


def advance(weight, second, received, fields, state):
    width = 2048
    return pl.pallas_call(
        advance_kernel,
        grid=(N // width,),
        in_specs=[
            pl.BlockSpec(memory_space=pltpu.SMEM),
            pl.BlockSpec(memory_space=pltpu.SMEM),
            pl.BlockSpec((6, 8, width), lambda p: (0, 0, p)),
            pl.BlockSpec((5, 8, width), lambda p: (0, 0, p)),
            pl.BlockSpec((6, 8, width), lambda p: (0, 0, p)),
        ],
        out_specs=pl.BlockSpec((6, 8, width), lambda p: (0, 0, p)),
        out_shape=jax.ShapeDtypeStruct((6, 8, N), jnp.float32),
        cost_estimate=pl.CostEstimate(flops=22 * 8 * N, bytes_accessed=23 * 8 * N * 4, transcendentals=0),
        name="advance",
    )(weight, second, received, fields, state)


def exchanged(value):
    return lax.all_to_all(value, "col", split_axis=0, concat_axis=0, tiled=True)


def body(convergence, lens_weight, rays_in):
    y, z = lax.axis_index("col"), lax.axis_index("row")
    rows = convergence.reshape(8, 16, 64, 256)
    sent, summed, returned = [], [], []
    for chunk in range(CHUNKS):
        sent.append(forward(rows, chunk))
    partial = None
    for chunk in range(CHUNKS):
        arrived = exchanged(sent[chunk])
        partial = row_stage(arrived, chunk, y, z, partial)
        if chunk % GROUP == GROUP - 1:
            summed.append(lax.psum_scatter(partial, "row", scatter_dimension=0, tiled=True))
            partial = None
    for group in range(CHUNKS // GROUP):
        returned.append(exchanged(summed[group]))
    fields, state = final_stage(returned, rows, lens_weight, rays_in)
    received = lax.ppermute(state, "shell", [(0, 1)])
    second = lax.axis_index("shell").astype(jnp.int32).reshape(1)
    return advance(lens_weight, second, received, fields, state)[None]


def solution(mesh):
    in_specs = (P("shell", ("row", "col"), None), P("shell"), P(None, ("row", "col"), None))
    out_specs = P("shell", None, ("row", "col"), None)
    return jax.shard_map(body, mesh=mesh, in_specs=in_specs, out_specs=out_specs, check_vma=False)
```

```python
import functools
import math

import jax
import jax.numpy as jnp
import ml_dtypes
import numpy as np
from jax import lax
from jax.experimental import pallas as pl
from jax.experimental.pallas import tpu as pltpu
from jax.sharding import PartitionSpec as P

N = 16384
CHUNKS = 4
HELD = 16 * CHUNKS
ROWS = 40
COLS = 16
DEEP = 8
LANES = 4
STEP = 2.0 * math.pi / N


def halves(table):
    table = np.asarray(table, np.float32)
    high = table.astype(ml_dtypes.bfloat16)
    low = (table - high.astype(np.float32)).astype(ml_dtypes.bfloat16)
    return high, low


def right_table(table):
    high, low = halves(table)
    return np.concatenate([high, high, low], axis=-2)


def left_table(table):
    high, low = halves(table)
    return np.concatenate([high, high, low], axis=-1)


def turns(first, second, length, sign):
    whole = np.outer(first, second) % length
    angle = sign * 2.0 * np.pi * whole / length
    return np.cos(angle), np.sin(angle)


def complex_right(first, second, length, sign):
    cosine, sine = turns(first, second, length, sign)
    return np.block([[cosine, sine], [-sine, cosine]])


def forward_tables():
    t = np.array([4 * y + k for k in range(CHUNKS) for y in range(COLS)])
    cosine, sine = turns(t, np.arange(64), 64, -1)
    high, low = halves(np.concatenate([cosine, sine], axis=0))
    first = np.concatenate([high, low], axis=1)
    twist = np.stack(turns(t, np.arange(256), N, -1)).astype(np.float32)
    second = right_table(complex_right(np.arange(256), np.arange(128), 256, -1))
    return first, twist, second


def row_tables():
    k = np.arange(128)
    grid = np.stack([right_table(complex_right(k, k + 128 * j, 1024, -1)) for j in range(8)])
    twist = np.zeros((8, 32, 128), np.float32)
    waves = np.zeros((8, 40, 128), np.float32)
    for j in range(8):
        base = k + 128 * j
        cosine, sine = turns(np.arange(16), base, N, -1)
        twist[j, 0::2], twist[j, 1::2] = cosine, sine
        for a in range(16):
            signed = base + 1024 * a - (N if a >= 8 else 0)
            wave = (2.0 * np.pi / N * signed).astype(np.float32)
            waves[j, a] = wave
            waves[j, 16 + a] = wave * wave
        waves[j, 32] = (base != 0).astype(np.float32)
    back = np.zeros((8, 16, 128), np.float32)
    for z in range(8):
        cosine, sine = turns(np.arange(8) - 128 * z, k, 1024, 1)
        back[z, 0::2], back[z, 1::2] = cosine * (-2.0 / N / N), sine * (-2.0 / N / N)
    cosine, sine = turns(k, k, 128, 1)
    left = left_table(np.block([[cosine, -sine], [sine, cosine]]))
    return grid, twist, waves, back, left


def final_tables():
    t = np.array([4 * y + k for k in range(4) for y in range(16)])
    first = right_table(complex_right(np.arange(128), np.arange(256), 256, 1))
    twist = np.stack(turns(t, np.arange(256), N, 1)).astype(np.float32)
    cosine, sine = turns(np.arange(64), t, 64, 1)
    second = left_table(np.concatenate([cosine, -sine], axis=1))
    bins = 64 * np.arange(128)[None, :] + t[:, None]
    wave = (2.0 * np.pi / N * bins).astype(np.float32)
    weight = np.where(bins == 0, 1.0, 2.0).astype(np.float32)
    scales = np.stack([weight, weight * wave, weight * wave * wave]).astype(np.float32)
    return first, twist, second, scales


def dot(left, right):
    return jnp.dot(left, right, preferred_element_type=jnp.float32)


def split(value):
    high = value.astype(jnp.bfloat16)
    low = (value - high.astype(jnp.float32)).astype(jnp.bfloat16)
    return high, low


def times(x, cosine, sine):
    return x[0] * cosine - x[1] * sine, x[0] * sine + x[1] * cosine


def plus(x, y):
    return x[0] + y[0], x[1] + y[1]


def minus(x, y):
    return x[0] - y[0], x[1] - y[1]


def quarter(x, sign):
    return (-x[1], x[0]) if sign > 0 else (x[1], -x[0])


def turned(x, eighths, sign):
    eighths %= 16
    if eighths == 0:
        return x
    if eighths == 4:
        return quarter(x, sign)
    if eighths == 2 or eighths == 6:
        root = math.sqrt(0.5)
        real, imaginary = x if eighths == 2 else quarter(x, sign)
        if sign > 0:
            return (real - imaginary) * root, (real + imaginary) * root
        return (real + imaginary) * root, (imaginary - real) * root
    angle = sign * 2.0 * math.pi * eighths / 16
    return times(x, math.cos(angle), math.sin(angle))


def four(x, sign):
    a, b = plus(x[0], x[2]), minus(x[0], x[2])
    c, d = plus(x[1], x[3]), quarter(minus(x[1], x[3]), sign)
    return [plus(a, c), plus(b, d), minus(a, c), minus(b, d)]


def sixteen(x, sign):
    inner = [four([x[4 * p + q] for p in range(4)], sign) for q in range(4)]
    out = [None] * 16
    for a in range(4):
        outer = four([turned(inner[q][a], q * a, sign) for q in range(4)], sign)
        for b in range(4):
            out[a + 4 * b] = outer[b]
    return out


def eight(x, sign):
    even, odd = four(x[0::2], sign), four(x[1::2], sign)
    odd = [turned(odd[i], 2 * i, sign) for i in range(4)]
    return [plus(even[i], odd[i]) for i in range(4)] + [minus(even[i], odd[i]) for i in range(4)]


def forward_kernel(k_ref, first_ref, twist_ref, second_ref, o_ref, l_ref):
    for r in range(8):
        row = k_ref[r]
        a = dot(first_ref[...], jnp.concatenate([row, row], axis=0))
        real, imaginary = times((a[:HELD], a[HELD:]), twist_ref[0], twist_ref[1])
        high, low = split(jnp.concatenate([real, imaginary], axis=1))
        l_ref[pl.ds(r * HELD, HELD), :] = jnp.concatenate([high, low, high], axis=1)
    out = dot(l_ref[...], second_ref[...])
    for part in range(2):
        piece = out[:, 128 * part : 128 * part + 128].reshape(8, HELD, 128)
        o_ref[:, part] = jnp.swapaxes(piece, 0, 1)


def whole(shape):
    return pl.BlockSpec(shape, lambda *_: (0,) * len(shape), pipeline_mode=pl.Buffered(1))


def forward(rows):
    first, twist, second = (jnp.asarray(x) for x in forward_tables())
    return pl.pallas_call(
        forward_kernel,
        grid=(16,),
        in_specs=[
            pl.BlockSpec((8, None, 64, 256), lambda v: (0, v, 0, 0)),
            whole(first.shape),
            whole(twist.shape),
            whole(second.shape),
        ],
        out_specs=pl.BlockSpec((HELD, 2, 8, 128), lambda v: (0, 0, v, 0)),
        out_shape=jax.ShapeDtypeStruct((HELD, 2, 128, 128), jnp.float32),
        scratch_shapes=[pltpu.VMEM((8 * HELD, 1536), jnp.bfloat16)],
        compiler_params=pltpu.CompilerParams(vmem_limit_bytes=40 << 20),
        cost_estimate=pl.CostEstimate(flops=2 * 128 * HELD * 2500 * 256, bytes_accessed=8 << 20, transcendentals=0),
        name="forward",
    )(rows, first, twist, second)


def filter_rows(z_ref, position, x_ref_twist, waves_ref, squares_ref, s_ref, q_ref):
    group, j = position // 8, position % 8
    for part in range(2):
        rows = pl.ds(pl.multiple_of(group * 16 + part * 8, 8), 8)
        square = squares_ref[rows, :]
        values = []
        for v in range(16):
            x = z_ref[v * 16 + part * 8 : v * 16 + part * 8 + 8, :128], z_ref[v * 16 + part * 8 : v * 16 + part * 8 + 8, 128:]
            if v:
                x = times(x, x_ref_twist[j, 2 * v : 2 * v + 1, :], x_ref_twist[j, 2 * v + 1 : 2 * v + 2, :])
            values.append(x)
        values = sixteen(values, -1)
        q_ref[j, 0, rows, :] = values[8][0] + jnp.where(square == 0.0, values[0][0], 0.0)
        q_ref[j, 1, rows, :] = values[8][1] + jnp.where(square == 0.0, values[0][1], 0.0)
        totals = None
        for a in range(16):
            wave = waves_ref[j, a : a + 1, :]
            below = waves_ref[j, 16 + a : 17 + a, :] + square
            if a == 0:
                scale = jnp.where(below > 0.0, 1.0 / jnp.where(below > 0.0, below, 1.0), 0.0)
            else:
                scale = 1.0 / below
            if a == 8:
                scale = scale * waves_ref[j, 32:33, :]
            real, imaginary = values[a][0] * scale, values[a][1] * scale
            terms = [real, imaginary, real * wave, imaginary * wave]
            totals = terms if totals is None else [p + t for p, t in zip(totals, terms)]
        for f in range(4):
            s_ref[f, j, rows, :] = totals[f]


def row_chunk(x_ref, squares_ref, grid_ref, twist_ref, waves_ref, back_ref, left_ref, o_ref, l_ref, z0_ref, z1_ref, s_ref, q_ref, g_ref, r_ref, between):
    def arrange(v, _):
        rows = pl.ds(pl.multiple_of(v * 8, 8), 8)
        real = x_ref[:, 0, rows, :].reshape(128, 128)
        imaginary = x_ref[:, 1, rows, :].reshape(128, 128)
        high, low = split(jnp.concatenate([real.T, imaginary.T], axis=1))
        l_ref[:, v] = jnp.concatenate([high, low, high], axis=1).reshape(8, 16, 768)
        return 0

    lax.fori_loop(0, 16, arrange, 0)

    def multiply(position, z_ref):
        z_ref[...] = dot(l_ref[position // 8].reshape(256, 768), grid_ref[position % 8])

    def filtered(position, z_ref):
        filter_rows(z_ref, position, twist_ref, waves_ref, squares_ref, s_ref, q_ref)

    multiply(0, z0_ref)

    def pair(h, _):
        multiply(2 * h + 1, z1_ref)
        filtered(2 * h, z0_ref)
        multiply(jnp.minimum(2 * h + 2, 63), z0_ref)
        filtered(2 * h + 1, z1_ref)
        return 0

    def segment(g, _):
        lax.fori_loop(0, 4, lambda h, c: pair(4 * g + h, c), 0)
        between(g)
        return 0

    lax.fori_loop(0, 7, segment, 0)
    lax.fori_loop(28, 32, pair, 0)

    def unfold(group, _):
        rows = pl.ds(pl.multiple_of(group * 16, 16), 16)
        for f in range(2):
            values = eight([(s_ref[2 * f, j, rows, :], s_ref[2 * f + 1, j, rows, :]) for j in range(8)], 1)
            for i in range(8):
                real, imaginary = times(values[i], back_ref[2 * i : 2 * i + 1, :], back_ref[2 * i + 1 : 2 * i + 2, :])
                high, low = split(jnp.concatenate([real, imaginary], axis=1))
                g_ref[8 * f + i, rows, :] = jnp.concatenate([high, low, high], axis=1)
        return 0

    lax.fori_loop(0, 8, unfold, 0)

    def outward(q, _):
        for e in range(4):
            result = lax.dot_general(left_ref[...], g_ref[4 * q + e], (((1,), (1,)), ((), ())), preferred_element_type=jnp.float32)
            r_ref[2 * e] = result[:128]
            r_ref[2 * e + 1] = result[128:]
        o_ref[:, pl.ds(pl.multiple_of(q * 8, 8), 8), :] = jnp.swapaxes(r_ref[...], 0, 1)
        return 0

    lax.fori_loop(0, 4, outward, 0)
    lines = jnp.zeros((8, 128), jnp.float32)
    for part in range(2):
        line = q_ref[0, part].T[0:1] * (1.0 / N / N)
        place = lax.broadcasted_iota(jnp.int32, (8, 128), 0) == part
        lines = lines + jnp.where(place, jnp.broadcast_to(line, (8, 128)), 0.0)
    o_ref[:, 32:40, :] = jnp.broadcast_to(lines[None], (128, 8, 128))


def exchange_kernel(
    sent_ref, squares_ref, grid_ref, twist_ref, waves_ref, back_ref, left_ref, o_ref,
    arrived_ref, partial_ref, slot_ref, reduced_ref, landed_ref, l_ref, z0_ref, z1_ref, s_ref, q_ref, g_ref, r_ref,
    own_sem, in_send, in_recv, ring_send, ring_recv, back_send, back_recv,
):
    y, z = lax.axis_index("col"), lax.axis_index("row")
    right, left = lax.rem(z + 1, DEEP), lax.rem(z + DEEP - 1, DEEP)
    barrier = pltpu.get_barrier_semaphore()

    def greet(d, _):
        pl.semaphore_signal(barrier, inc=1, device_id={"col": lax.rem(y + d, COLS)}, device_id_type=pl.DeviceIdType.MESH)
        return 0

    lax.fori_loop(1, COLS, greet, 0)
    for neighbour in (left, right):
        pl.semaphore_signal(barrier, inc=1, device_id={"row": neighbour}, device_id_type=pl.DeviceIdType.MESH)
    pl.semaphore_wait(barrier, COLS + 1)

    def inward(k, d):
        peer = lax.rem(y + d, COLS)
        return pltpu.make_async_remote_copy(
            sent_ref.at[k, peer], arrived_ref.at[k, y], in_send.at[k, d], in_recv.at[k, d],
            device_id={"col": peer}, device_id_type=pl.DeviceIdType.MESH,
        )

    def own(k):
        return pltpu.make_async_copy(sent_ref.at[k, y], arrived_ref.at[k, y], own_sem.at[k])

    def homeward(k, d):
        peer = lax.rem(y + d, COLS)
        rows = pl.ds(pl.multiple_of(k * ROWS, 8), ROWS)
        return pltpu.make_async_remote_copy(
            reduced_ref.at[k, peer], landed_ref.at[y, rows], back_send.at[k, d], back_recv.at[k, d],
            device_id={"col": peer}, device_id_type=pl.DeviceIdType.MESH,
        )

    def share(block, lane):
        return pl.ds(lax.rem(block + 2 * DEEP, DEEP) * COLS + 4 * lane, 4)

    def ring(k, lane, s, source):
        return pltpu.make_async_remote_copy(
            source, slot_ref.at[k, lane, s], ring_send.at[k, lane, s], ring_recv.at[k, lane, s],
            device_id={"row": right if lane % 2 == 0 else left}, device_id_type=pl.DeviceIdType.MESH,
        )

    def open_ring(k):
        for lane in range(LANES):
            block = z - 1 if lane % 2 == 0 else z + 1
            ring(k, lane, 0, partial_ref.at[k, share(block, lane)]).start()

    def step(k, s):
        for lane in range(LANES):
            ring(k, lane, s, slot_ref.at[k, lane, s]).wait_recv()
            block = z - s - 2 if lane % 2 == 0 else z + s + 2
            total = slot_ref[k, lane, s] + partial_ref[k, share(block, lane)]

            @pl.when(s < DEEP - 2)
            def _():
                slot_ref[k, lane, s] = total
                ring(k, lane, s + 1, slot_ref.at[k, lane, s]).start()

            @pl.when(s == DEEP - 2)
            def _():
                reduced_ref[k, 4 * lane : 4 * lane + 4] = total

    def close_ring(k):
        landed_ref[y, pl.ds(pl.multiple_of(k * ROWS, 8), ROWS), :] = reduced_ref[k, y]

        def give(d, _):
            homeward(k, d).start()
            return 0

        lax.fori_loop(1, COLS, give, 0)

    def launch(k, _):
        own(k).start()

        def give(d, _):
            inward(k, d).start()
            return 0

        lax.fori_loop(1, COLS, give, 0)
        return 0

    lax.fori_loop(0, CHUNKS, launch, 0)

    def chunk(k, _):
        own(k).wait()

        def take(d, _):
            inward(k, d).wait_recv()
            return 0

        lax.fori_loop(1, COLS, take, 0)

        @pl.when(k > 0)
        def _():
            open_ring(k - 1)

        def between(s):
            @pl.when(k > 0)
            def _():
                step(k - 1, s)

        row_chunk(
            arrived_ref.at[k], squares_ref.at[k], grid_ref, twist_ref, waves_ref, back_ref, left_ref,
            partial_ref.at[k], l_ref, z0_ref, z1_ref, s_ref, q_ref, g_ref, r_ref, between,
        )

        @pl.when(k > 0)
        def _():
            close_ring(k - 1)

        return 0

    lax.fori_loop(0, CHUNKS, chunk, 0)
    open_ring(CHUNKS - 1)

    def last(s, _):
        step(CHUNKS - 1, s)
        return 0

    lax.fori_loop(0, DEEP - 1, last, 0)
    close_ring(CHUNKS - 1)

    def settle(k, _):
        def one(d, _):
            inward(k, d).wait_send()
            homeward(k, d).wait_send()
            homeward(k, d).wait_recv()
            return 0

        lax.fori_loop(1, COLS, one, 0)

        def two(s, _):
            for lane in range(LANES):
                ring(k, lane, s, slot_ref.at[k, lane, s]).wait_send()
            return 0

        lax.fori_loop(0, DEEP - 1, two, 0)
        return 0

    lax.fori_loop(0, CHUNKS, settle, 0)
    o_ref[...] = landed_ref[...]


def exchange(sent, y, z):
    tables = [jnp.asarray(x) for x in row_tables()]
    tables[3] = lax.dynamic_index_in_dim(tables[3], z, 0, keepdims=False)
    t = 4 * y + jnp.arange(CHUNKS, dtype=jnp.int32)
    wave = STEP * (64 * jnp.arange(128, dtype=jnp.int32)[None, :] + t[:, None]).astype(jnp.float32)
    squares = jnp.broadcast_to((wave * wave)[:, :, None], (CHUNKS, 128, 128))
    vmem = pl.BlockSpec(memory_space=pltpu.VMEM)
    return pl.pallas_call(
        exchange_kernel,
        in_specs=[pl.BlockSpec(memory_space=pl.ANY)] + [vmem] * (1 + len(tables)),
        out_specs=vmem,
        out_shape=jax.ShapeDtypeStruct((COLS, CHUNKS * ROWS, 128), jnp.float32),
        scratch_shapes=[
            pltpu.VMEM((CHUNKS, COLS, 2, 128, 128), jnp.float32),
            pltpu.VMEM((CHUNKS, 128, ROWS, 128), jnp.float32),
            pltpu.VMEM((CHUNKS, LANES, DEEP - 1, 4, ROWS, 128), jnp.float32),
            pltpu.VMEM((CHUNKS, COLS, ROWS, 128), jnp.float32),
            pltpu.VMEM((COLS, CHUNKS * ROWS, 128), jnp.float32),
            pltpu.VMEM((8, 16, 16, 768), jnp.bfloat16),
            pltpu.VMEM((256, 256), jnp.float32),
            pltpu.VMEM((256, 256), jnp.float32),
            pltpu.VMEM((4, 8, 128, 128), jnp.float32),
            pltpu.VMEM((8, 2, 128, 128), jnp.float32),
            pltpu.VMEM((16, 128, 768), jnp.bfloat16),
            pltpu.VMEM((8, 128, 128), jnp.float32),
            pltpu.SemaphoreType.DMA((CHUNKS,)),
            pltpu.SemaphoreType.DMA((CHUNKS, COLS)),
            pltpu.SemaphoreType.DMA((CHUNKS, COLS)),
            pltpu.SemaphoreType.DMA((CHUNKS, LANES, DEEP - 1)),
            pltpu.SemaphoreType.DMA((CHUNKS, LANES, DEEP - 1)),
            pltpu.SemaphoreType.DMA((CHUNKS, COLS)),
            pltpu.SemaphoreType.DMA((CHUNKS, COLS)),
        ],
        compiler_params=pltpu.CompilerParams(vmem_limit_bytes=63 << 20, collective_id=0, has_side_effects=True),
        name="exchange",
    )(sent.reshape(CHUNKS, COLS, 2, 128, 128), squares, *tables)


def final_kernel(*refs):
    y_ref, w_ref, state_ref, k_ref, first_ref, twist_ref, second_ref, scales_ref, o_ref, n_ref, a_ref, r_ref, f_ref = refs
    for k in range(CHUNKS):
        for q in range(5):
            block = jnp.swapaxes(y_ref[:, ROWS * k + 8 * q : ROWS * k + 8 * q + 8, :], 0, 1)
            a_ref[8 * q : 8 * q + 8, 16 * k : 16 * k + 16, :] = block

    def synthesis(pairs):
        high, low = split(jnp.concatenate([jnp.concatenate(p, axis=1) for p in pairs], axis=0))
        out = dot(jnp.concatenate([high, low, high], axis=1), first_ref[...])
        results = []
        for f in range(len(pairs)):
            x = out[64 * f : 64 * f + 64, :256], out[64 * f : 64 * f + 64, 256:]
            high, low = split(jnp.concatenate(times(x, twist_ref[0], twist_ref[1]), axis=0))
            results.append(dot(second_ref[...], jnp.concatenate([high, low, high], axis=0)))
        return results

    weight = scales_ref[0]
    r_ref[...] = synthesis([(a_ref[32] * weight, a_ref[33] * weight)])[0]
    sign = (1 - 2 * (lax.broadcasted_iota(jnp.int32, (64, 256), 1) % 2)).astype(jnp.float32)

    def ray(i, _):
        base = a_ref[2 * i], a_ref[2 * i + 1]
        slope = a_ref[16 + 2 * i], a_ref[17 + 2 * i]
        one, wave, square = scales_ref[0], scales_ref[1], scales_ref[2]
        alpha_rows, alpha_cols, curve_cols, curve_mixed = synthesis(
            [
                (-slope[1] * one, slope[0] * one),
                (-base[1] * wave, base[0] * wave),
                (-base[0] * square, -base[1] * square),
                (-slope[0] * wave, -slope[1] * wave),
            ]
        )
        kappa = k_ref[i].astype(jnp.float32)
        edge = sign * (jnp.sum(kappa * sign) * (1.0 / N))
        curve_rows = 2.0 * (kappa - edge - r_ref[...]) - curve_cols
        for f, field in enumerate([alpha_rows, alpha_cols, curve_rows, curve_cols, curve_mixed]):
            f_ref[f, i] = field
        return 0

    lax.fori_loop(0, 8, ray, 0)

    def emit(g, _):
        blocks = [jnp.swapaxes(f_ref[f, :, pl.ds(pl.multiple_of(8 * g, 8), 8), :], 0, 1) for f in range(5)]
        for v in range(8):
            place = pl.ds(pl.multiple_of((8 * g + v) * 256, 256), 256)
            fields = [block[v] for block in blocks]
            for f in range(5):
                o_ref[f, :, place] = fields[f]
            for e, value in enumerate(moved([state_ref[e, :, place] for e in range(6)], fields, w_ref[0])):
                n_ref[e, :, place] = value
        return 0

    lax.fori_loop(0, 8, emit, 0)


def moved(state, fields, w):
    rows, cols, mixed = w * fields[2], w * fields[3], w * fields[4]
    upper_left, upper_right, lower_left, lower_right = state[2:]
    return [
        state[0] - w * fields[0],
        state[1] - w * fields[1],
        upper_left - (rows * upper_left + mixed * lower_left),
        upper_right - (rows * upper_right + mixed * lower_right),
        lower_left - (mixed * upper_left + cols * lower_left),
        lower_right - (mixed * upper_right + cols * lower_right),
    ]


def final_stage(returned, rows, weight, state):
    tables = [jnp.asarray(x) for x in final_tables()]
    return pl.pallas_call(
        final_kernel,
        grid=(1,),
        in_specs=[whole((COLS, CHUNKS * ROWS, 128))]
        + [pl.BlockSpec(memory_space=pltpu.SMEM), whole((6, 8, N))]
        + [pl.BlockSpec((8, None, 64, 256), lambda v: (0, 0, 0, 0))]
        + [whole(x.shape) for x in tables],
        out_specs=[whole((5, 8, N)), whole((6, 8, N))],
        out_shape=[jax.ShapeDtypeStruct((5, 8, N), jnp.float32), jax.ShapeDtypeStruct((6, 8, N), jnp.float32)],
        scratch_shapes=[
            pltpu.VMEM((40, 64, 128), jnp.float32),
            pltpu.VMEM((64, 256), jnp.float32),
            pltpu.VMEM((5, 8, 64, 256), jnp.float32),
        ],
        compiler_params=pltpu.CompilerParams(vmem_limit_bytes=40 << 20),
        cost_estimate=pl.CostEstimate(flops=2 * 16384 * 65536, bytes_accessed=8 << 20, transcendentals=0),
        name="final_stage",
    )(returned, weight, state, rows, *tables)


def advance_kernel(w_ref, second_ref, s_ref, f_ref, n_ref, o_ref):
    last = second_ref[0] == 1
    values = moved([s_ref[e] for e in range(6)], [f_ref[f] for f in range(5)], w_ref[0])
    for e in range(6):
        o_ref[e] = jnp.where(last, values[e], n_ref[e])


def advance(weight, second, received, fields, state):
    width = 2048
    return pl.pallas_call(
        advance_kernel,
        grid=(N // width,),
        in_specs=[
            pl.BlockSpec(memory_space=pltpu.SMEM),
            pl.BlockSpec(memory_space=pltpu.SMEM),
            pl.BlockSpec((6, 8, width), lambda p: (0, 0, p)),
            pl.BlockSpec((5, 8, width), lambda p: (0, 0, p)),
            pl.BlockSpec((6, 8, width), lambda p: (0, 0, p)),
        ],
        out_specs=pl.BlockSpec((6, 8, width), lambda p: (0, 0, p)),
        out_shape=jax.ShapeDtypeStruct((6, 8, N), jnp.float32),
        cost_estimate=pl.CostEstimate(flops=22 * 8 * N, bytes_accessed=23 * 8 * N * 4, transcendentals=0),
        name="advance",
    )(weight, second, received, fields, state)


def body(convergence, lens_weight, rays_in):
    y, z = lax.axis_index("col"), lax.axis_index("row")
    rows = convergence.reshape(8, 16, 64, 256)
    returned = exchange(forward(rows), y, z)
    fields, state = final_stage(returned, rows, lens_weight, rays_in)
    received = lax.ppermute(state, "shell", [(0, 1)])
    second = lax.axis_index("shell").astype(jnp.int32).reshape(1)
    return advance(lens_weight, second, received, fields, state)[None]


def solution(mesh):
    in_specs = (P("shell", ("row", "col"), None), P("shell"), P(None, ("row", "col"), None))
    out_specs = P("shell", None, ("row", "col"), None)
    return jax.shard_map(body, mesh=mesh, in_specs=in_specs, out_specs=out_specs, check_vma=False)
```

```python
import functools
import math

import jax
import jax.numpy as jnp
import ml_dtypes
import numpy as np
from jax import lax
from jax.experimental import pallas as pl
from jax.experimental.pallas import tpu as pltpu
from jax.sharding import PartitionSpec as P

N = 16384
CHUNKS = 4
HELD = 16 * CHUNKS
ROWS = 40
COLS = 16
DEEP = 8
LANES = 4
STEP = 2.0 * math.pi / N


def halves(table):
    table = np.asarray(table, np.float32)
    high = table.astype(ml_dtypes.bfloat16)
    low = (table - high.astype(np.float32)).astype(ml_dtypes.bfloat16)
    return high, low


def right_table(table):
    high, low = halves(table)
    return np.concatenate([high, high, low], axis=-2)


def left_table(table):
    high, low = halves(table)
    return np.concatenate([high, high, low], axis=-1)


def turns(first, second, length, sign):
    whole = np.outer(first, second) % length
    angle = sign * 2.0 * np.pi * whole / length
    return np.cos(angle), np.sin(angle)


def complex_right(first, second, length, sign):
    cosine, sine = turns(first, second, length, sign)
    return np.block([[cosine, sine], [-sine, cosine]])


def forward_tables():
    t = np.array([4 * y + k for k in range(CHUNKS) for y in range(COLS)])
    cosine, sine = turns(t, np.arange(64), 64, -1)
    high, low = halves(np.concatenate([cosine, sine], axis=0))
    first = np.concatenate([high, low], axis=1)
    twist = np.stack(turns(t, np.arange(256), N, -1)).astype(np.float32)
    second = right_table(complex_right(np.arange(256), np.arange(128), 256, -1))
    return first, twist, second


def row_tables():
    k = np.arange(128)
    grid = np.stack([right_table(complex_right(k, k + 128 * j, 1024, -1)) for j in range(8)])
    twist = np.zeros((8, 32, 128), np.float32)
    waves = np.zeros((8, 40, 128), np.float32)
    for j in range(8):
        base = k + 128 * j
        cosine, sine = turns(np.arange(16), base, N, -1)
        twist[j, 0::2], twist[j, 1::2] = cosine, sine
        for a in range(16):
            signed = base + 1024 * a - (N if a >= 8 else 0)
            wave = (2.0 * np.pi / N * signed).astype(np.float32)
            waves[j, a] = wave
            waves[j, 16 + a] = wave * wave
        waves[j, 32] = (base != 0).astype(np.float32)
    back = np.zeros((8, 16, 128), np.float32)
    for z in range(8):
        cosine, sine = turns(np.arange(8) - 128 * z, k, 1024, 1)
        back[z, 0::2], back[z, 1::2] = cosine * (-2.0 / N / N), sine * (-2.0 / N / N)
    cosine, sine = turns(k, k, 128, 1)
    left = left_table(np.block([[cosine, -sine], [sine, cosine]]))
    return grid, twist, waves, back, left


def final_tables():
    t = np.array([4 * y + k for k in range(4) for y in range(16)])
    first = right_table(complex_right(np.arange(128), np.arange(256), 256, 1))
    twist = np.stack(turns(t, np.arange(256), N, 1)).astype(np.float32)
    cosine, sine = turns(np.arange(64), t, 64, 1)
    second = left_table(np.concatenate([cosine, -sine], axis=1))
    bins = 64 * np.arange(128)[None, :] + t[:, None]
    wave = (2.0 * np.pi / N * bins).astype(np.float32)
    weight = np.where(bins == 0, 1.0, 2.0).astype(np.float32)
    scales = np.stack([weight, weight * wave, weight * wave * wave]).astype(np.float32)
    return first, twist, second, scales


def dot(left, right):
    return jnp.dot(left, right, preferred_element_type=jnp.float32)


def split(value):
    high = value.astype(jnp.bfloat16)
    low = (value - high.astype(jnp.float32)).astype(jnp.bfloat16)
    return high, low


def times(x, cosine, sine):
    return x[0] * cosine - x[1] * sine, x[0] * sine + x[1] * cosine


def plus(x, y):
    return x[0] + y[0], x[1] + y[1]


def minus(x, y):
    return x[0] - y[0], x[1] - y[1]


def quarter(x, sign):
    return (-x[1], x[0]) if sign > 0 else (x[1], -x[0])


def turned(x, eighths, sign):
    eighths %= 16
    if eighths == 0:
        return x
    if eighths == 4:
        return quarter(x, sign)
    if eighths == 2 or eighths == 6:
        root = math.sqrt(0.5)
        real, imaginary = x if eighths == 2 else quarter(x, sign)
        if sign > 0:
            return (real - imaginary) * root, (real + imaginary) * root
        return (real + imaginary) * root, (imaginary - real) * root
    angle = sign * 2.0 * math.pi * eighths / 16
    return times(x, math.cos(angle), math.sin(angle))


def four(x, sign):
    a, b = plus(x[0], x[2]), minus(x[0], x[2])
    c, d = plus(x[1], x[3]), quarter(minus(x[1], x[3]), sign)
    return [plus(a, c), plus(b, d), minus(a, c), minus(b, d)]


def sixteen(x, sign):
    inner = [four([x[4 * p + q] for p in range(4)], sign) for q in range(4)]
    out = [None] * 16
    for a in range(4):
        outer = four([turned(inner[q][a], q * a, sign) for q in range(4)], sign)
        for b in range(4):
            out[a + 4 * b] = outer[b]
    return out


def eight(x, sign):
    even, odd = four(x[0::2], sign), four(x[1::2], sign)
    odd = [turned(odd[i], 2 * i, sign) for i in range(4)]
    return [plus(even[i], odd[i]) for i in range(4)] + [minus(even[i], odd[i]) for i in range(4)]


def forward_kernel(k_ref, first_ref, twist_ref, second_ref, o_ref, l_ref):
    for r in range(8):
        row = k_ref[r]
        a = dot(first_ref[...], jnp.concatenate([row, row], axis=0))
        real, imaginary = times((a[:HELD], a[HELD:]), twist_ref[0], twist_ref[1])
        high, low = split(jnp.concatenate([real, imaginary], axis=1))
        l_ref[pl.ds(r * HELD, HELD), :] = jnp.concatenate([high, low, high], axis=1)
    out = dot(l_ref[...], second_ref[...])
    for part in range(2):
        piece = out[:, 128 * part : 128 * part + 128].reshape(8, HELD, 128)
        o_ref[:, part] = jnp.swapaxes(piece, 0, 1)


def whole(shape):
    return pl.BlockSpec(shape, lambda *_: (0,) * len(shape), pipeline_mode=pl.Buffered(1))


def forward(rows):
    first, twist, second = (jnp.asarray(x) for x in forward_tables())
    return pl.pallas_call(
        forward_kernel,
        grid=(16,),
        in_specs=[
            pl.BlockSpec((8, None, 64, 256), lambda v: (0, v, 0, 0)),
            whole(first.shape),
            whole(twist.shape),
            whole(second.shape),
        ],
        out_specs=pl.BlockSpec((HELD, 2, 8, 128), lambda v: (0, 0, v, 0)),
        out_shape=jax.ShapeDtypeStruct((HELD, 2, 128, 128), jnp.float32),
        scratch_shapes=[pltpu.VMEM((8 * HELD, 1536), jnp.bfloat16)],
        compiler_params=pltpu.CompilerParams(vmem_limit_bytes=40 << 20),
        cost_estimate=pl.CostEstimate(flops=2 * 128 * HELD * 2500 * 256, bytes_accessed=8 << 20, transcendentals=0),
        name="forward",
    )(rows, first, twist, second)


def filter_rows(z_ref, position, x_ref_twist, waves_ref, squares_ref, s_ref, q_ref):
    group, j = position // 8, position % 8
    for part in range(2):
        rows = pl.ds(pl.multiple_of(group * 16 + part * 8, 8), 8)
        square = squares_ref[rows, :]
        values = []
        for v in range(16):
            x = z_ref[v * 16 + part * 8 : v * 16 + part * 8 + 8, :128], z_ref[v * 16 + part * 8 : v * 16 + part * 8 + 8, 128:]
            if v:
                x = times(x, x_ref_twist[j, 2 * v : 2 * v + 1, :], x_ref_twist[j, 2 * v + 1 : 2 * v + 2, :])
            values.append(x)
        values = sixteen(values, -1)
        q_ref[j, 0, rows, :] = values[8][0] + jnp.where(square == 0.0, values[0][0], 0.0)
        q_ref[j, 1, rows, :] = values[8][1] + jnp.where(square == 0.0, values[0][1], 0.0)
        totals = None
        for a in range(16):
            wave = waves_ref[j, a : a + 1, :]
            below = waves_ref[j, 16 + a : 17 + a, :] + square
            if a == 0:
                scale = jnp.where(below > 0.0, 1.0 / jnp.where(below > 0.0, below, 1.0), 0.0)
            else:
                scale = 1.0 / below
            if a == 8:
                scale = scale * waves_ref[j, 32:33, :]
            real, imaginary = values[a][0] * scale, values[a][1] * scale
            terms = [real, imaginary, real * wave, imaginary * wave]
            totals = terms if totals is None else [p + t for p, t in zip(totals, terms)]
        for f in range(4):
            s_ref[f, j, rows, :] = totals[f]


def row_chunk(x_ref, squares_ref, grid_ref, twist_ref, waves_ref, back_ref, left_ref, o_ref, l_ref, z0_ref, z1_ref, s_ref, q_ref, g_ref, r_ref, between):
    def arrange(v, _):
        rows = pl.ds(pl.multiple_of(v * 8, 8), 8)
        real = x_ref[:, 0, rows, :].reshape(128, 128)
        imaginary = x_ref[:, 1, rows, :].reshape(128, 128)
        high, low = split(jnp.concatenate([real.T, imaginary.T], axis=1))
        l_ref[:, v] = jnp.concatenate([high, low, high], axis=1).reshape(8, 16, 768)
        return 0

    lax.fori_loop(0, 16, arrange, 0)

    def multiply(position, z_ref):
        z_ref[...] = dot(l_ref[position // 8].reshape(256, 768), grid_ref[position % 8])

    def filtered(position, z_ref):
        filter_rows(z_ref, position, twist_ref, waves_ref, squares_ref, s_ref, q_ref)

    multiply(0, z0_ref)

    def pair(h, _):
        multiply(2 * h + 1, z1_ref)
        filtered(2 * h, z0_ref)
        multiply(jnp.minimum(2 * h + 2, 63), z0_ref)
        filtered(2 * h + 1, z1_ref)
        return 0

    def segment(g, _):
        lax.fori_loop(0, 4, lambda h, c: pair(4 * g + h, c), 0)
        between(g)
        return 0

    lax.fori_loop(0, 7, segment, 0)
    lax.fori_loop(28, 32, pair, 0)

    def unfold(group, _):
        rows = pl.ds(pl.multiple_of(group * 16, 16), 16)
        for f in range(2):
            values = eight([(s_ref[2 * f, j, rows, :], s_ref[2 * f + 1, j, rows, :]) for j in range(8)], 1)
            for i in range(8):
                real, imaginary = times(values[i], back_ref[2 * i : 2 * i + 1, :], back_ref[2 * i + 1 : 2 * i + 2, :])
                high, low = split(jnp.concatenate([real, imaginary], axis=1))
                g_ref[8 * f + i, rows, :] = jnp.concatenate([high, low, high], axis=1)
        return 0

    lax.fori_loop(0, 8, unfold, 0)

    def outward(q, _):
        for e in range(4):
            result = lax.dot_general(left_ref[...], g_ref[4 * q + e], (((1,), (1,)), ((), ())), preferred_element_type=jnp.float32)
            r_ref[2 * e] = result[:128]
            r_ref[2 * e + 1] = result[128:]
        o_ref[:, pl.ds(pl.multiple_of(q * 8, 8), 8), :] = jnp.swapaxes(r_ref[...], 0, 1)
        return 0

    lax.fori_loop(0, 4, outward, 0)
    lines = jnp.zeros((8, 128), jnp.float32)
    for part in range(2):
        line = q_ref[0, part].T[0:1] * (1.0 / N / N)
        place = lax.broadcasted_iota(jnp.int32, (8, 128), 0) == part
        lines = lines + jnp.where(place, jnp.broadcast_to(line, (8, 128)), 0.0)
    o_ref[:, 32:40, :] = jnp.broadcast_to(lines[None], (128, 8, 128))


def exchange_kernel(
    sent_ref, squares_ref, grid_ref, twist_ref, waves_ref, back_ref, left_ref, o_ref,
    arrived_ref, partial_ref, slot_ref, reduced_ref, landed_ref, l_ref, z0_ref, z1_ref, s_ref, q_ref, g_ref, r_ref,
    own_sem, in_send, in_recv, ring_send, ring_recv, back_send, back_recv,
):
    y, z = lax.axis_index("col"), lax.axis_index("row")
    right, left = lax.rem(z + 1, DEEP), lax.rem(z + DEEP - 1, DEEP)
    barrier = pltpu.get_barrier_semaphore()

    def greet(d, _):
        pl.semaphore_signal(barrier, inc=1, device_id={"col": lax.rem(y + d, COLS)}, device_id_type=pl.DeviceIdType.MESH)
        return 0

    lax.fori_loop(1, COLS, greet, 0)
    for neighbour in (left, right):
        pl.semaphore_signal(barrier, inc=1, device_id={"row": neighbour}, device_id_type=pl.DeviceIdType.MESH)
    pl.semaphore_wait(barrier, COLS + 1)

    def inward(k, d):
        peer = lax.rem(y + d, COLS)
        return pltpu.make_async_remote_copy(
            sent_ref.at[k, peer], arrived_ref.at[k, y], in_send.at[k, d], in_recv.at[k, d],
            device_id={"col": peer}, device_id_type=pl.DeviceIdType.MESH,
        )

    def own(k):
        return pltpu.make_async_copy(sent_ref.at[k, y], arrived_ref.at[k, y], own_sem.at[k])

    def homeward(k, d):
        peer = lax.rem(y + d, COLS)
        rows = pl.ds(pl.multiple_of(k * ROWS, 8), ROWS)
        return pltpu.make_async_remote_copy(
            reduced_ref.at[k, peer], landed_ref.at[y, rows], back_send.at[k, d], back_recv.at[k, d],
            device_id={"col": peer}, device_id_type=pl.DeviceIdType.MESH,
        )

    def share(block, lane):
        return pl.ds(lax.rem(block + 2 * DEEP, DEEP) * COLS + 4 * lane, 4)

    def ring(k, lane, s, source):
        return pltpu.make_async_remote_copy(
            source, slot_ref.at[k, lane, s], ring_send.at[k, lane, s], ring_recv.at[k, lane, s],
            device_id={"row": right if lane % 2 == 0 else left}, device_id_type=pl.DeviceIdType.MESH,
        )

    def open_ring(k):
        for lane in range(LANES):
            block = z - 1 if lane % 2 == 0 else z + 1
            ring(k, lane, 0, partial_ref.at[k, share(block, lane)]).start()

    def step(k, s):
        for lane in range(LANES):
            ring(k, lane, s, slot_ref.at[k, lane, s]).wait_recv()
            block = z - s - 2 if lane % 2 == 0 else z + s + 2
            total = slot_ref[k, lane, s] + partial_ref[k, share(block, lane)]

            @pl.when(s < DEEP - 2)
            def _():
                slot_ref[k, lane, s] = total
                ring(k, lane, s + 1, slot_ref.at[k, lane, s]).start()

            @pl.when(s == DEEP - 2)
            def _():
                reduced_ref[k, 4 * lane : 4 * lane + 4] = total

    def close_ring(k):
        landed_ref[y, pl.ds(pl.multiple_of(k * ROWS, 8), ROWS), :] = reduced_ref[k, y]

        def give(d, _):
            homeward(k, d).start()
            return 0

        lax.fori_loop(1, COLS, give, 0)

    def launch(k, _):
        own(k).start()

        def give(d, _):
            inward(k, d).start()
            return 0

        lax.fori_loop(1, COLS, give, 0)
        return 0

    launch(0, 0)

    def chunk(k, _):
        own(k).wait()

        def take(d, _):
            inward(k, d).wait_recv()
            return 0

        lax.fori_loop(1, COLS, take, 0)

        @pl.when(k < CHUNKS - 1)
        def _():
            launch(k + 1, 0)

        @pl.when(k > 0)
        def _():
            open_ring(k - 1)

        def between(s):
            @pl.when(k > 0)
            def _():
                step(k - 1, s)

        row_chunk(
            arrived_ref.at[k], squares_ref.at[k], grid_ref, twist_ref, waves_ref, back_ref, left_ref,
            partial_ref.at[k], l_ref, z0_ref, z1_ref, s_ref, q_ref, g_ref, r_ref, between,
        )

        @pl.when(k > 0)
        def _():
            close_ring(k - 1)

        return 0

    lax.fori_loop(0, CHUNKS, chunk, 0)
    open_ring(CHUNKS - 1)

    def last(s, _):
        step(CHUNKS - 1, s)
        return 0

    lax.fori_loop(0, DEEP - 1, last, 0)
    close_ring(CHUNKS - 1)

    def settle(k, _):
        def one(d, _):
            inward(k, d).wait_send()
            homeward(k, d).wait_send()
            homeward(k, d).wait_recv()
            return 0

        lax.fori_loop(1, COLS, one, 0)

        def two(s, _):
            for lane in range(LANES):
                ring(k, lane, s, slot_ref.at[k, lane, s]).wait_send()
            return 0

        lax.fori_loop(0, DEEP - 1, two, 0)
        return 0

    lax.fori_loop(0, CHUNKS, settle, 0)
    o_ref[...] = landed_ref[...]


def exchange(sent, y, z):
    tables = [jnp.asarray(x) for x in row_tables()]
    tables[3] = lax.dynamic_index_in_dim(tables[3], z, 0, keepdims=False)
    t = 4 * y + jnp.arange(CHUNKS, dtype=jnp.int32)
    wave = STEP * (64 * jnp.arange(128, dtype=jnp.int32)[None, :] + t[:, None]).astype(jnp.float32)
    squares = jnp.broadcast_to((wave * wave)[:, :, None], (CHUNKS, 128, 128))
    vmem = pl.BlockSpec(memory_space=pltpu.VMEM)
    return pl.pallas_call(
        exchange_kernel,
        in_specs=[pl.BlockSpec(memory_space=pl.ANY)] + [vmem] * (1 + len(tables)),
        out_specs=vmem,
        out_shape=jax.ShapeDtypeStruct((COLS, CHUNKS * ROWS, 128), jnp.float32),
        scratch_shapes=[
            pltpu.VMEM((CHUNKS, COLS, 2, 128, 128), jnp.float32),
            pltpu.VMEM((CHUNKS, 128, ROWS, 128), jnp.float32),
            pltpu.VMEM((CHUNKS, LANES, DEEP - 1, 4, ROWS, 128), jnp.float32),
            pltpu.VMEM((CHUNKS, COLS, ROWS, 128), jnp.float32),
            pltpu.VMEM((COLS, CHUNKS * ROWS, 128), jnp.float32),
            pltpu.VMEM((8, 16, 16, 768), jnp.bfloat16),
            pltpu.VMEM((256, 256), jnp.float32),
            pltpu.VMEM((256, 256), jnp.float32),
            pltpu.VMEM((4, 8, 128, 128), jnp.float32),
            pltpu.VMEM((8, 2, 128, 128), jnp.float32),
            pltpu.VMEM((16, 128, 768), jnp.bfloat16),
            pltpu.VMEM((8, 128, 128), jnp.float32),
            pltpu.SemaphoreType.DMA((CHUNKS,)),
            pltpu.SemaphoreType.DMA((CHUNKS, COLS)),
            pltpu.SemaphoreType.DMA((CHUNKS, COLS)),
            pltpu.SemaphoreType.DMA((CHUNKS, LANES, DEEP - 1)),
            pltpu.SemaphoreType.DMA((CHUNKS, LANES, DEEP - 1)),
            pltpu.SemaphoreType.DMA((CHUNKS, COLS)),
            pltpu.SemaphoreType.DMA((CHUNKS, COLS)),
        ],
        compiler_params=pltpu.CompilerParams(vmem_limit_bytes=63 << 20, collective_id=0, has_side_effects=True),
        name="exchange",
    )(sent.reshape(CHUNKS, COLS, 2, 128, 128), squares, *tables)


def final_kernel(*refs):
    y_ref, w_ref, state_ref, k_ref, first_ref, twist_ref, second_ref, scales_ref, o_ref, a_ref, r_ref, f_ref, held_ref, send_sem, recv_sem = refs
    shell = lax.axis_index("shell")
    barrier = pltpu.get_barrier_semaphore()
    pl.semaphore_signal(barrier, inc=1, device_id={"shell": 1 - shell}, device_id_type=pl.DeviceIdType.MESH)
    pl.semaphore_wait(barrier, 1)
    for k in range(CHUNKS):
        for q in range(5):
            block = jnp.swapaxes(y_ref[:, ROWS * k + 8 * q : ROWS * k + 8 * q + 8, :], 0, 1)
            a_ref[8 * q : 8 * q + 8, 16 * k : 16 * k + 16, :] = block

    def synthesis(pairs):
        high, low = split(jnp.concatenate([jnp.concatenate(p, axis=1) for p in pairs], axis=0))
        out = dot(jnp.concatenate([high, low, high], axis=1), first_ref[...])
        results = []
        for f in range(len(pairs)):
            x = out[64 * f : 64 * f + 64, :256], out[64 * f : 64 * f + 64, 256:]
            high, low = split(jnp.concatenate(times(x, twist_ref[0], twist_ref[1]), axis=0))
            results.append(dot(second_ref[...], jnp.concatenate([high, low, high], axis=0)))
        return results

    weight = scales_ref[0]
    r_ref[...] = synthesis([(a_ref[32] * weight, a_ref[33] * weight)])[0]
    sign = (1 - 2 * (lax.broadcasted_iota(jnp.int32, (64, 256), 1) % 2)).astype(jnp.float32)

    def ray(i, _):
        base = a_ref[2 * i], a_ref[2 * i + 1]
        slope = a_ref[16 + 2 * i], a_ref[17 + 2 * i]
        one, wave, square = scales_ref[0], scales_ref[1], scales_ref[2]
        alpha_rows, alpha_cols, curve_cols, curve_mixed = synthesis(
            [
                (-slope[1] * one, slope[0] * one),
                (-base[1] * wave, base[0] * wave),
                (-base[0] * square, -base[1] * square),
                (-slope[0] * wave, -slope[1] * wave),
            ]
        )
        kappa = k_ref[i].astype(jnp.float32)
        edge = sign * (jnp.sum(kappa * sign) * (1.0 / N))
        curve_rows = 2.0 * (kappa - edge - r_ref[...]) - curve_cols
        for f, field in enumerate([alpha_rows, alpha_cols, curve_rows, curve_cols, curve_mixed]):
            f_ref[f, i] = field
        return 0

    lax.fori_loop(0, 8, ray, 0)

    def passed(g):
        part = (slice(None), slice(None), pl.ds(pl.multiple_of(2048 * g, 2048), 2048))
        return pltpu.make_async_remote_copy(
            o_ref.at[part], held_ref.at[part], send_sem.at[g], recv_sem.at[g],
            device_id={"shell": 1 - shell}, device_id_type=pl.DeviceIdType.MESH,
        )

    def emit(g, source_ref):
        blocks = [jnp.swapaxes(f_ref[f, :, pl.ds(pl.multiple_of(8 * g, 8), 8), :], 0, 1) for f in range(5)]
        for v in range(8):
            place = pl.ds(pl.multiple_of((8 * g + v) * 256, 256), 256)
            fields = [block[v] for block in blocks]
            for e, value in enumerate(moved([source_ref[e, :, place] for e in range(6)], fields, w_ref[0])):
                o_ref[e, :, place] = value

    def opening(g, _):
        emit(g, state_ref)
        passed(g).start()
        return 0

    def closing(g, _):
        passed(g).wait_recv()
        emit(g, held_ref)
        return 0

    def settled(g, _):
        passed(g).wait_send()
        return 0

    @pl.when(shell == 0)
    def _():
        lax.fori_loop(0, 8, opening, 0)
        lax.fori_loop(0, 8, settled, 0)

    @pl.when(shell == 1)
    def _():
        lax.fori_loop(0, 8, closing, 0)


def moved(state, fields, w):
    rows, cols, mixed = w * fields[2], w * fields[3], w * fields[4]
    upper_left, upper_right, lower_left, lower_right = state[2:]
    return [
        state[0] - w * fields[0],
        state[1] - w * fields[1],
        upper_left - (rows * upper_left + mixed * lower_left),
        upper_right - (rows * upper_right + mixed * lower_right),
        lower_left - (mixed * upper_left + cols * lower_left),
        lower_right - (mixed * upper_right + cols * lower_right),
    ]


def final_stage(returned, rows, weight, state):
    tables = [jnp.asarray(x) for x in final_tables()]
    vmem = pl.BlockSpec(memory_space=pltpu.VMEM)
    return pl.pallas_call(
        final_kernel,
        in_specs=[vmem, pl.BlockSpec(memory_space=pltpu.SMEM)] + [vmem] * (2 + len(tables)),
        out_specs=vmem,
        out_shape=jax.ShapeDtypeStruct((6, 8, N), jnp.float32),
        scratch_shapes=[
            pltpu.VMEM((40, 64, 128), jnp.float32),
            pltpu.VMEM((64, 256), jnp.float32),
            pltpu.VMEM((5, 8, 64, 256), jnp.float32),
            pltpu.VMEM((6, 8, N), jnp.float32),
            pltpu.SemaphoreType.DMA((8,)),
            pltpu.SemaphoreType.DMA((8,)),
        ],
        compiler_params=pltpu.CompilerParams(vmem_limit_bytes=40 << 20, collective_id=1, has_side_effects=True),
        name="final_stage",
    )(returned, weight, state, rows, *tables)


def body(convergence, lens_weight, rays_in):
    y, z = lax.axis_index("col"), lax.axis_index("row")
    rows = convergence.reshape(8, 16, 64, 256)
    returned = exchange(forward(rows), y, z)
    kept = convergence.reshape(8, 16, N)[:, 0].reshape(8, 64, 256)
    return final_stage(returned, kept, lens_weight, rays_in)[None]


def solution(mesh):
    in_specs = (P("shell", ("row", "col"), None), P("shell"), P(None, ("row", "col"), None))
    out_specs = P("shell", None, ("row", "col"), None)
    return jax.shard_map(body, mesh=mesh, in_specs=in_specs, out_specs=out_specs, check_vma=False)
```

```python
import functools
import math

import jax
import jax.numpy as jnp
import ml_dtypes
import numpy as np
from jax import lax
from jax.experimental import pallas as pl
from jax.experimental.pallas import tpu as pltpu
from jax.sharding import PartitionSpec as P

N = 16384
CHUNKS = 4
HELD = 16 * CHUNKS
ROWS = 40
COLS = 16
DEEP = 8
LANES = 8
STEP = 2.0 * math.pi / N


def halves(table):
    table = np.asarray(table, np.float32)
    high = table.astype(ml_dtypes.bfloat16)
    low = (table - high.astype(np.float32)).astype(ml_dtypes.bfloat16)
    return high, low


def right_table(table):
    high, low = halves(table)
    return np.concatenate([high, high, low], axis=-2)


def left_table(table):
    high, low = halves(table)
    return np.concatenate([high, high, low], axis=-1)


def turns(first, second, length, sign):
    whole = np.outer(first, second) % length
    angle = sign * 2.0 * np.pi * whole / length
    return np.cos(angle), np.sin(angle)


def complex_right(first, second, length, sign):
    cosine, sine = turns(first, second, length, sign)
    return np.block([[cosine, sine], [-sine, cosine]])


def forward_tables():
    t = np.array([4 * y + k for k in range(CHUNKS) for y in range(COLS)])
    cosine, sine = turns(t, np.arange(64), 64, -1)
    high, low = halves(np.concatenate([cosine, sine], axis=0))
    first = np.concatenate([high, low], axis=1)
    twist = np.stack(turns(t, np.arange(256), N, -1)).astype(np.float32)
    second = right_table(complex_right(np.arange(256), np.arange(128), 256, -1))
    return first, twist, second


def row_tables():
    k = np.arange(128)
    grid = np.stack([right_table(complex_right(k, k + 128 * j, 1024, -1)) for j in range(8)])
    twist = np.zeros((8, 32, 128), np.float32)
    waves = np.zeros((8, 40, 128), np.float32)
    for j in range(8):
        base = k + 128 * j
        cosine, sine = turns(np.arange(16), base, N, -1)
        twist[j, 0::2], twist[j, 1::2] = cosine, sine
        for a in range(16):
            signed = base + 1024 * a - (N if a >= 8 else 0)
            wave = (2.0 * np.pi / N * signed).astype(np.float32)
            waves[j, a] = wave
            waves[j, 16 + a] = wave * wave
        waves[j, 32] = (base != 0).astype(np.float32)
    back = np.zeros((8, 16, 128), np.float32)
    for z in range(8):
        cosine, sine = turns(np.arange(8) - 128 * z, k, 1024, 1)
        back[z, 0::2], back[z, 1::2] = cosine * (-2.0 / N / N), sine * (-2.0 / N / N)
    cosine, sine = turns(k, k, 128, 1)
    left = left_table(np.block([[cosine, -sine], [sine, cosine]]))
    return grid, twist, waves, back, left


def final_tables():
    t = np.array([4 * y + k for k in range(4) for y in range(16)])
    first = right_table(complex_right(np.arange(128), np.arange(256), 256, 1))
    twist = np.stack(turns(t, np.arange(256), N, 1)).astype(np.float32)
    cosine, sine = turns(np.arange(64), t, 64, 1)
    second = left_table(np.concatenate([cosine, -sine], axis=1))
    bins = 64 * np.arange(128)[None, :] + t[:, None]
    wave = (2.0 * np.pi / N * bins).astype(np.float32)
    weight = np.where(bins == 0, 1.0, 2.0).astype(np.float32)
    scales = np.stack([weight, weight * wave, weight * wave * wave]).astype(np.float32)
    return first, twist, second, scales


def dot(left, right):
    return jnp.dot(left, right, preferred_element_type=jnp.float32)


def split(value):
    high = value.astype(jnp.bfloat16)
    low = (value - high.astype(jnp.float32)).astype(jnp.bfloat16)
    return high, low


def times(x, cosine, sine):
    return x[0] * cosine - x[1] * sine, x[0] * sine + x[1] * cosine


def plus(x, y):
    return x[0] + y[0], x[1] + y[1]


def minus(x, y):
    return x[0] - y[0], x[1] - y[1]


def quarter(x, sign):
    return (-x[1], x[0]) if sign > 0 else (x[1], -x[0])


def turned(x, eighths, sign):
    eighths %= 16
    if eighths == 0:
        return x
    if eighths == 4:
        return quarter(x, sign)
    if eighths == 2 or eighths == 6:
        root = math.sqrt(0.5)
        real, imaginary = x if eighths == 2 else quarter(x, sign)
        if sign > 0:
            return (real - imaginary) * root, (real + imaginary) * root
        return (real + imaginary) * root, (imaginary - real) * root
    angle = sign * 2.0 * math.pi * eighths / 16
    return times(x, math.cos(angle), math.sin(angle))


def four(x, sign):
    a, b = plus(x[0], x[2]), minus(x[0], x[2])
    c, d = plus(x[1], x[3]), quarter(minus(x[1], x[3]), sign)
    return [plus(a, c), plus(b, d), minus(a, c), minus(b, d)]


def sixteen(x, sign):
    inner = [four([x[4 * p + q] for p in range(4)], sign) for q in range(4)]
    out = [None] * 16
    for a in range(4):
        outer = four([turned(inner[q][a], q * a, sign) for q in range(4)], sign)
        for b in range(4):
            out[a + 4 * b] = outer[b]
    return out


def eight(x, sign):
    even, odd = four(x[0::2], sign), four(x[1::2], sign)
    odd = [turned(odd[i], 2 * i, sign) for i in range(4)]
    return [plus(even[i], odd[i]) for i in range(4)] + [minus(even[i], odd[i]) for i in range(4)]


def forward_kernel(k_ref, first_ref, twist_ref, second_ref, o_ref, l_ref):
    for r in range(8):
        row = k_ref[r]
        a = dot(first_ref[...], jnp.concatenate([row, row], axis=0))
        real, imaginary = times((a[:HELD], a[HELD:]), twist_ref[0], twist_ref[1])
        high, low = split(jnp.concatenate([real, imaginary], axis=1))
        l_ref[pl.ds(r * HELD, HELD), :] = jnp.concatenate([high, low, high], axis=1)
    out = dot(l_ref[...], second_ref[...])
    for part in range(2):
        piece = out[:, 128 * part : 128 * part + 128].reshape(8, HELD, 128)
        o_ref[:, part] = jnp.swapaxes(piece, 0, 1)


def whole(shape):
    return pl.BlockSpec(shape, lambda *_: (0,) * len(shape), pipeline_mode=pl.Buffered(1))


def forward(rows):
    first, twist, second = (jnp.asarray(x) for x in forward_tables())
    return pl.pallas_call(
        forward_kernel,
        grid=(16,),
        in_specs=[
            pl.BlockSpec((8, None, 64, 256), lambda v: (0, v, 0, 0)),
            whole(first.shape),
            whole(twist.shape),
            whole(second.shape),
        ],
        out_specs=pl.BlockSpec((HELD, 2, 8, 128), lambda v: (0, 0, v, 0)),
        out_shape=jax.ShapeDtypeStruct((HELD, 2, 128, 128), jnp.float32),
        scratch_shapes=[pltpu.VMEM((8 * HELD, 1536), jnp.bfloat16)],
        compiler_params=pltpu.CompilerParams(vmem_limit_bytes=62 << 20),
        cost_estimate=pl.CostEstimate(flops=2 * 128 * HELD * 2500 * 256, bytes_accessed=8 << 20, transcendentals=0),
        name="forward",
    )(rows, first, twist, second)


def filter_rows(z_ref, position, x_ref_twist, waves_ref, squares_ref, s_ref, q_ref):
    group, j = position // 8, position % 8
    for part in range(2):
        rows = pl.ds(pl.multiple_of(group * 16 + part * 8, 8), 8)
        square = squares_ref[rows, :]
        values = []
        for v in range(16):
            x = z_ref[v * 16 + part * 8 : v * 16 + part * 8 + 8, :128], z_ref[v * 16 + part * 8 : v * 16 + part * 8 + 8, 128:]
            if v:
                x = times(x, x_ref_twist[j, 2 * v : 2 * v + 1, :], x_ref_twist[j, 2 * v + 1 : 2 * v + 2, :])
            values.append(x)
        values = sixteen(values, -1)
        q_ref[j, 0, rows, :] = values[8][0] + jnp.where(square == 0.0, values[0][0], 0.0)
        q_ref[j, 1, rows, :] = values[8][1] + jnp.where(square == 0.0, values[0][1], 0.0)
        totals = None
        for a in range(16):
            wave = waves_ref[j, a : a + 1, :]
            below = waves_ref[j, 16 + a : 17 + a, :] + square
            if a == 0:
                scale = jnp.where(below > 0.0, 1.0 / jnp.where(below > 0.0, below, 1.0), 0.0)
            else:
                scale = 1.0 / below
            if a == 8:
                scale = scale * waves_ref[j, 32:33, :]
            real, imaginary = values[a][0] * scale, values[a][1] * scale
            terms = [real, imaginary, real * wave, imaginary * wave]
            totals = terms if totals is None else [p + t for p, t in zip(totals, terms)]
        for f in range(4):
            s_ref[f, j, rows, :] = totals[f]


def row_chunk(x_ref, squares_ref, grid_ref, twist_ref, waves_ref, back_ref, left_ref, o_ref, l_ref, z0_ref, z1_ref, s_ref, q_ref, g_ref, r_ref, between):
    def arrange(v, _):
        rows = pl.ds(pl.multiple_of(v * 8, 8), 8)
        real = x_ref[:, 0, rows, :].reshape(128, 128)
        imaginary = x_ref[:, 1, rows, :].reshape(128, 128)
        high, low = split(jnp.concatenate([real.T, imaginary.T], axis=1))
        l_ref[:, v] = jnp.concatenate([high, low, high], axis=1).reshape(8, 16, 768)
        return 0

    lax.fori_loop(0, 16, arrange, 0)

    def multiply(position, z_ref):
        z_ref[...] = dot(l_ref[position // 8].reshape(256, 768), grid_ref[position % 8])

    def filtered(position, z_ref):
        filter_rows(z_ref, position, twist_ref, waves_ref, squares_ref, s_ref, q_ref)

    multiply(0, z0_ref)

    def pair(h, _):
        multiply(2 * h + 1, z1_ref)
        filtered(2 * h, z0_ref)
        multiply(jnp.minimum(2 * h + 2, 63), z0_ref)
        filtered(2 * h + 1, z1_ref)
        return 0

    def segment(g, _):
        lax.fori_loop(0, 4, lambda h, c: pair(4 * g + h, c), 0)
        between(g)
        return 0

    lax.fori_loop(0, 7, segment, 0)
    lax.fori_loop(28, 32, pair, 0)

    def unfold(group, _):
        rows = pl.ds(pl.multiple_of(group * 16, 16), 16)
        for f in range(2):
            values = eight([(s_ref[2 * f, j, rows, :], s_ref[2 * f + 1, j, rows, :]) for j in range(8)], 1)
            for i in range(8):
                real, imaginary = times(values[i], back_ref[2 * i : 2 * i + 1, :], back_ref[2 * i + 1 : 2 * i + 2, :])
                high, low = split(jnp.concatenate([real, imaginary], axis=1))
                g_ref[8 * f + i, rows, :] = jnp.concatenate([high, low, high], axis=1)
        return 0

    lax.fori_loop(0, 8, unfold, 0)

    def outward(q, _):
        for e in range(4):
            result = lax.dot_general(left_ref[...], g_ref[4 * q + e], (((1,), (1,)), ((), ())), preferred_element_type=jnp.float32)
            r_ref[2 * e] = result[:128]
            r_ref[2 * e + 1] = result[128:]
        o_ref[:, pl.ds(pl.multiple_of(q * 8, 8), 8), :] = jnp.swapaxes(r_ref[...], 0, 1)
        return 0

    lax.fori_loop(0, 4, outward, 0)
    lines = jnp.zeros((8, 128), jnp.float32)
    for part in range(2):
        line = q_ref[0, part].T[0:1] * (1.0 / N / N)
        place = lax.broadcasted_iota(jnp.int32, (8, 128), 0) == part
        lines = lines + jnp.where(place, jnp.broadcast_to(line, (8, 128)), 0.0)
    o_ref[:, 32:40, :] = jnp.broadcast_to(lines[None], (128, 8, 128))


def exchange_kernel(
    sent_ref, squares_ref, grid_ref, twist_ref, waves_ref, back_ref, left_ref, o_ref,
    arrived_ref, partial_ref, slot_ref, reduced_ref, landed_ref, l_ref, z0_ref, z1_ref, s_ref, q_ref, g_ref, r_ref,
    own_sem, in_send, in_recv, ring_send, ring_recv, back_send, back_recv,
):
    y, z = lax.axis_index("col"), lax.axis_index("row")
    right, left = lax.rem(z + 1, DEEP), lax.rem(z + DEEP - 1, DEEP)
    barrier = pltpu.get_barrier_semaphore()

    def greet(d, _):
        pl.semaphore_signal(barrier, inc=1, device_id={"col": lax.rem(y + d, COLS)}, device_id_type=pl.DeviceIdType.MESH)
        return 0

    lax.fori_loop(1, COLS, greet, 0)
    for neighbour in (left, right):
        pl.semaphore_signal(barrier, inc=1, device_id={"row": neighbour}, device_id_type=pl.DeviceIdType.MESH)
    pl.semaphore_wait(barrier, COLS + 1)

    def inward(k, d):
        peer = lax.rem(y + d, COLS)
        return pltpu.make_async_remote_copy(
            sent_ref.at[k, peer], arrived_ref.at[k, y], in_send.at[k, d], in_recv.at[k, d],
            device_id={"col": peer}, device_id_type=pl.DeviceIdType.MESH,
        )

    def own(k):
        return pltpu.make_async_copy(sent_ref.at[k, y], arrived_ref.at[k, y], own_sem.at[k])

    def homeward(k, d):
        peer = lax.rem(y + d, COLS)
        rows = pl.ds(pl.multiple_of(k * ROWS, 8), ROWS)
        return pltpu.make_async_remote_copy(
            reduced_ref.at[k, peer], landed_ref.at[y, rows], back_send.at[k, d], back_recv.at[k, d],
            device_id={"col": peer}, device_id_type=pl.DeviceIdType.MESH,
        )

    def share(block, lane):
        return pl.ds(lax.rem(block + 2 * DEEP, DEEP) * COLS + 2 * lane, 2)

    def ring(k, lane, s, source):
        return pltpu.make_async_remote_copy(
            source, slot_ref.at[k, lane, s], ring_send.at[k, lane, s], ring_recv.at[k, lane, s],
            device_id={"row": right if lane % 2 == 0 else left}, device_id_type=pl.DeviceIdType.MESH,
        )

    def open_ring(k):
        for lane in range(LANES):
            block = z - 1 if lane % 2 == 0 else z + 1
            ring(k, lane, 0, partial_ref.at[k, share(block, lane)]).start()

    def step(k, s):
        for lane in range(LANES):
            ring(k, lane, s, slot_ref.at[k, lane, s]).wait_recv()
            block = z - s - 2 if lane % 2 == 0 else z + s + 2
            total = slot_ref[k, lane, s] + partial_ref[k, share(block, lane)]

            @pl.when(s < DEEP - 2)
            def _():
                slot_ref[k, lane, s] = total
                ring(k, lane, s + 1, slot_ref.at[k, lane, s]).start()

            @pl.when(s == DEEP - 2)
            def _():
                reduced_ref[k, 2 * lane : 2 * lane + 2] = total

    def close_ring(k):
        landed_ref[y, pl.ds(pl.multiple_of(k * ROWS, 8), ROWS), :] = reduced_ref[k, y]

        def give(d, _):
            homeward(k, d).start()
            return 0

        lax.fori_loop(1, COLS, give, 0)

    def launch(k, _):
        own(k).start()

        def give(d, _):
            inward(k, d).start()
            return 0

        lax.fori_loop(1, COLS, give, 0)
        return 0

    launch(0, 0)

    def chunk(k, _):
        own(k).wait()

        def take(d, _):
            inward(k, d).wait_recv()
            return 0

        lax.fori_loop(1, COLS, take, 0)

        @pl.when(k == 0)
        def _():
            launch(1, 0)

        @pl.when(k > 0)
        def _():
            open_ring(k - 1)

        def between(g):
            @pl.when((k > 0) & (g % 2 == 0))
            def _():
                step(k - 1, g // 2)

            @pl.when((k > 1) & (g % 2 == 1))
            def _():
                step(k - 2, 4 + g // 2)

            @pl.when((k < CHUNKS - 2) & (g == 5))
            def _():
                launch(k + 2, 0)

        row_chunk(
            arrived_ref.at[k], squares_ref.at[k], grid_ref, twist_ref, waves_ref, back_ref, left_ref,
            partial_ref.at[k], l_ref, z0_ref, z1_ref, s_ref, q_ref, g_ref, r_ref, between,
        )

        @pl.when(k > 1)
        def _():
            close_ring(k - 2)

        return 0

    lax.fori_loop(0, CHUNKS, chunk, 0)
    open_ring(CHUNKS - 1)

    def both(s, _):
        step(CHUNKS - 2, 4 + s)
        step(CHUNKS - 1, s)
        return 0

    def last(s, _):
        step(CHUNKS - 1, s)
        return 0

    lax.fori_loop(0, 3, both, 0)
    close_ring(CHUNKS - 2)
    lax.fori_loop(3, DEEP - 1, last, 0)
    close_ring(CHUNKS - 1)

    def settle(k, _):
        def one(d, _):
            inward(k, d).wait_send()
            homeward(k, d).wait_send()
            homeward(k, d).wait_recv()
            return 0

        lax.fori_loop(1, COLS, one, 0)

        def two(s, _):
            for lane in range(LANES):
                ring(k, lane, s, slot_ref.at[k, lane, s]).wait_send()
            return 0

        lax.fori_loop(0, DEEP - 1, two, 0)
        return 0

    lax.fori_loop(0, CHUNKS, settle, 0)
    o_ref[...] = landed_ref[...]


def exchange(sent, y, z):
    tables = [jnp.asarray(x) for x in row_tables()]
    tables[3] = lax.dynamic_index_in_dim(tables[3], z, 0, keepdims=False)
    t = 4 * y + jnp.arange(CHUNKS, dtype=jnp.int32)
    wave = STEP * (64 * jnp.arange(128, dtype=jnp.int32)[None, :] + t[:, None]).astype(jnp.float32)
    squares = jnp.broadcast_to((wave * wave)[:, :, None], (CHUNKS, 128, 128))
    vmem = pl.BlockSpec(memory_space=pltpu.VMEM)
    return pl.pallas_call(
        exchange_kernel,
        in_specs=[pl.BlockSpec(memory_space=pl.ANY)] + [vmem] * (1 + len(tables)),
        out_specs=vmem,
        out_shape=jax.ShapeDtypeStruct((COLS, CHUNKS * ROWS, 128), jnp.float32),
        scratch_shapes=[
            pltpu.VMEM((CHUNKS, COLS, 2, 128, 128), jnp.float32),
            pltpu.VMEM((CHUNKS, 128, ROWS, 128), jnp.float32),
            pltpu.VMEM((CHUNKS, LANES, DEEP - 1, 2, ROWS, 128), jnp.float32),
            pltpu.VMEM((CHUNKS, COLS, ROWS, 128), jnp.float32),
            pltpu.VMEM((COLS, CHUNKS * ROWS, 128), jnp.float32),
            pltpu.VMEM((8, 16, 16, 768), jnp.bfloat16),
            pltpu.VMEM((256, 256), jnp.float32),
            pltpu.VMEM((256, 256), jnp.float32),
            pltpu.VMEM((4, 8, 128, 128), jnp.float32),
            pltpu.VMEM((8, 2, 128, 128), jnp.float32),
            pltpu.VMEM((16, 128, 768), jnp.bfloat16),
            pltpu.VMEM((8, 128, 128), jnp.float32),
            pltpu.SemaphoreType.DMA((CHUNKS,)),
            pltpu.SemaphoreType.DMA((CHUNKS, COLS)),
            pltpu.SemaphoreType.DMA((CHUNKS, COLS)),
            pltpu.SemaphoreType.DMA((CHUNKS, LANES, DEEP - 1)),
            pltpu.SemaphoreType.DMA((CHUNKS, LANES, DEEP - 1)),
            pltpu.SemaphoreType.DMA((CHUNKS, COLS)),
            pltpu.SemaphoreType.DMA((CHUNKS, COLS)),
        ],
        compiler_params=pltpu.CompilerParams(vmem_limit_bytes=63 << 20, collective_id=0, has_side_effects=True),
        name="exchange",
    )(sent.reshape(CHUNKS, COLS, 2, 128, 128), squares, *tables)


def final_kernel(*refs):
    y_ref, w_ref, state_hbm, rows_hbm, first_ref, twist_ref, second_ref, scales_ref, o_ref, a_ref, r_ref, f_ref, held_ref, send_sem, recv_sem, load_sem, k_ref, kept_sem = refs
    kept = pltpu.make_async_copy(rows_hbm.at[:, 0], k_ref, kept_sem)
    kept.start()
    shell = lax.axis_index("shell")
    barrier = pltpu.get_barrier_semaphore()
    pl.semaphore_signal(barrier, inc=1, device_id={"shell": 1 - shell}, device_id_type=pl.DeviceIdType.MESH)
    pl.semaphore_wait(barrier, 1)
    loaded = pltpu.make_async_copy(state_hbm, held_ref, load_sem)

    @pl.when(shell == 0)
    def _():
        loaded.start()

    for k in range(CHUNKS):
        for q in range(5):
            block = jnp.swapaxes(y_ref[:, ROWS * k + 8 * q : ROWS * k + 8 * q + 8, :], 0, 1)
            a_ref[8 * q : 8 * q + 8, 16 * k : 16 * k + 16, :] = block

    def synthesis(pairs):
        high, low = split(jnp.concatenate([jnp.concatenate(p, axis=1) for p in pairs], axis=0))
        out = dot(jnp.concatenate([high, low, high], axis=1), first_ref[...])
        results = []
        for f in range(len(pairs)):
            x = out[64 * f : 64 * f + 64, :256], out[64 * f : 64 * f + 64, 256:]
            high, low = split(jnp.concatenate(times(x, twist_ref[0], twist_ref[1]), axis=0))
            results.append(dot(second_ref[...], jnp.concatenate([high, low, high], axis=0)))
        return results

    weight = scales_ref[0]
    r_ref[...] = synthesis([(a_ref[32] * weight, a_ref[33] * weight)])[0]
    sign = (1 - 2 * (lax.broadcasted_iota(jnp.int32, (64, 256), 1) % 2)).astype(jnp.float32)

    def ray(i, _):
        base = a_ref[2 * i], a_ref[2 * i + 1]
        slope = a_ref[16 + 2 * i], a_ref[17 + 2 * i]
        one, wave, square = scales_ref[0], scales_ref[1], scales_ref[2]
        alpha_rows, alpha_cols, curve_cols, curve_mixed = synthesis(
            [
                (-slope[1] * one, slope[0] * one),
                (-base[1] * wave, base[0] * wave),
                (-base[0] * square, -base[1] * square),
                (-slope[0] * wave, -slope[1] * wave),
            ]
        )
        kappa = k_ref[i].astype(jnp.float32)
        edge = sign * (jnp.sum(kappa * sign) * (1.0 / N))
        curve_rows = 2.0 * (kappa - edge - r_ref[...]) - curve_cols
        for f, field in enumerate([alpha_rows, alpha_cols, curve_rows, curve_cols, curve_mixed]):
            f_ref[f, i] = field
        return 0

    kept.wait()
    lax.fori_loop(0, 8, ray, 0)

    def passed(g):
        part = (slice(None), slice(None), pl.ds(pl.multiple_of(2048 * g, 2048), 2048))
        return pltpu.make_async_remote_copy(
            o_ref.at[part], held_ref.at[part], send_sem.at[g], recv_sem.at[g],
            device_id={"shell": 1 - shell}, device_id_type=pl.DeviceIdType.MESH,
        )

    def emit(g, source_ref):
        blocks = [jnp.swapaxes(f_ref[f, :, pl.ds(pl.multiple_of(8 * g, 8), 8), :], 0, 1) for f in range(5)]
        for v in range(8):
            place = pl.ds(pl.multiple_of((8 * g + v) * 256, 256), 256)
            fields = [block[v] for block in blocks]
            for e, value in enumerate(moved([source_ref[e, :, place] for e in range(6)], fields, w_ref[0])):
                o_ref[e, :, place] = value

    def opening(g, _):
        emit(g, held_ref)
        passed(g).start()
        return 0

    def closing(g, _):
        passed(g).wait_recv()
        emit(g, held_ref)
        return 0

    def settled(g, _):
        passed(g).wait_send()
        return 0

    @pl.when(shell == 0)
    def _():
        loaded.wait()
        lax.fori_loop(0, 8, opening, 0)
        lax.fori_loop(0, 8, settled, 0)

    @pl.when(shell == 1)
    def _():
        lax.fori_loop(0, 8, closing, 0)


def moved(state, fields, w):
    rows, cols, mixed = w * fields[2], w * fields[3], w * fields[4]
    upper_left, upper_right, lower_left, lower_right = state[2:]
    return [
        state[0] - w * fields[0],
        state[1] - w * fields[1],
        upper_left - (rows * upper_left + mixed * lower_left),
        upper_right - (rows * upper_right + mixed * lower_right),
        lower_left - (mixed * upper_left + cols * lower_left),
        lower_right - (mixed * upper_right + cols * lower_right),
    ]


def final_stage(returned, rows, weight, state):
    tables = [jnp.asarray(x) for x in final_tables()]
    vmem = pl.BlockSpec(memory_space=pltpu.VMEM)
    return pl.pallas_call(
        final_kernel,
        in_specs=[vmem, pl.BlockSpec(memory_space=pltpu.SMEM), pl.BlockSpec(memory_space=pl.ANY), pl.BlockSpec(memory_space=pl.ANY)]
        + [vmem] * len(tables),
        out_specs=vmem,
        out_shape=jax.ShapeDtypeStruct((6, 8, N), jnp.float32),
        scratch_shapes=[
            pltpu.VMEM((40, 64, 128), jnp.float32),
            pltpu.VMEM((64, 256), jnp.float32),
            pltpu.VMEM((5, 8, 64, 256), jnp.float32),
            pltpu.VMEM((6, 8, N), jnp.float32),
            pltpu.SemaphoreType.DMA((8,)),
            pltpu.SemaphoreType.DMA((8,)),
            pltpu.SemaphoreType.DMA,
            pltpu.VMEM((8, 64, 256), jnp.bfloat16),
            pltpu.SemaphoreType.DMA,
        ],
        compiler_params=pltpu.CompilerParams(vmem_limit_bytes=40 << 20, collective_id=1, has_side_effects=True),
        name="final_stage",
    )(returned, weight, state, rows, *tables)


def body(convergence, lens_weight, rays_in):
    y, z = lax.axis_index("col"), lax.axis_index("row")
    rows = convergence.reshape(8, 16, 64, 256)
    returned = exchange(forward(rows), y, z)
    return final_stage(returned, rows, lens_weight, rays_in)[None]


def solution(mesh):
    in_specs = (P("shell", ("row", "col"), None), P("shell"), P(None, ("row", "col"), None))
    out_specs = P("shell", None, ("row", "col"), None)
    return jax.shard_map(body, mesh=mesh, in_specs=in_specs, out_specs=out_specs, check_vma=False)
```

```python
import functools
import math

import jax
import jax.numpy as jnp
import ml_dtypes
import numpy as np
from jax import lax
from jax.experimental import pallas as pl
from jax.experimental.pallas import tpu as pltpu
from jax.sharding import PartitionSpec as P

N = 16384
CHUNKS = 4
HELD = 16 * CHUNKS
ROWS = 40
COLS = 16
DEEP = 8
LANES = 8
STEP = 2.0 * math.pi / N


def halves(table):
    table = np.asarray(table, np.float32)
    high = table.astype(ml_dtypes.bfloat16)
    low = (table - high.astype(np.float32)).astype(ml_dtypes.bfloat16)
    return high, low


def right_table(table):
    high, low = halves(table)
    return np.concatenate([high, high, low], axis=-2)


def left_table(table):
    high, low = halves(table)
    return np.concatenate([high, high, low], axis=-1)


def turns(first, second, length, sign):
    whole = np.outer(first, second) % length
    angle = sign * 2.0 * np.pi * whole / length
    return np.cos(angle), np.sin(angle)


def complex_right(first, second, length, sign):
    cosine, sine = turns(first, second, length, sign)
    return np.block([[cosine, sine], [-sine, cosine]])


def forward_tables():
    t = np.array([4 * y + k for k in range(CHUNKS) for y in range(COLS)])
    cosine, sine = turns(t, np.arange(64), 64, -1)
    high, low = halves(np.concatenate([cosine, sine], axis=0))
    first = np.concatenate([high, low], axis=1)
    twist = np.stack(turns(t, np.arange(256), N, -1)).astype(np.float32)
    second = right_table(complex_right(np.arange(256), np.arange(128), 256, -1))
    return first, twist, second


def row_tables():
    k = np.arange(128)
    grid = np.stack([right_table(complex_right(k, k + 128 * j, 1024, -1)) for j in range(8)])
    twist = np.zeros((8, 32, 128), np.float32)
    waves = np.zeros((8, 40, 128), np.float32)
    for j in range(8):
        base = k + 128 * j
        cosine, sine = turns(np.arange(16), base, N, -1)
        twist[j, 0::2], twist[j, 1::2] = cosine, sine
        for a in range(16):
            signed = base + 1024 * a - (N if a >= 8 else 0)
            wave = (2.0 * np.pi / N * signed).astype(np.float32)
            waves[j, a] = wave
            waves[j, 16 + a] = wave * wave
        waves[j, 32] = (base != 0).astype(np.float32)
    back = np.zeros((8, 16, 128), np.float32)
    for z in range(8):
        cosine, sine = turns(np.arange(8) - 128 * z, k, 1024, 1)
        back[z, 0::2], back[z, 1::2] = cosine * (-2.0 / N / N), sine * (-2.0 / N / N)
    cosine, sine = turns(k, k, 128, 1)
    left = left_table(np.block([[cosine, -sine], [sine, cosine]]))
    return grid, twist, waves, back, left


def final_tables():
    t = np.array([4 * y + k for k in range(4) for y in range(16)])
    first = right_table(complex_right(np.arange(128), np.arange(256), 256, 1))
    twist = np.stack(turns(t, np.arange(256), N, 1)).astype(np.float32)
    cosine, sine = turns(np.arange(64), t, 64, 1)
    second = left_table(np.concatenate([cosine, -sine], axis=1))
    bins = 64 * np.arange(128)[None, :] + t[:, None]
    wave = (2.0 * np.pi / N * bins).astype(np.float32)
    weight = np.where(bins == 0, 1.0, 2.0).astype(np.float32)
    scales = np.stack([weight, weight * wave, weight * wave * wave]).astype(np.float32)
    return first, twist, second, scales


def dot(left, right):
    return jnp.dot(left, right, preferred_element_type=jnp.float32)


def split(value):
    high = value.astype(jnp.bfloat16)
    low = (value - high.astype(jnp.float32)).astype(jnp.bfloat16)
    return high, low


def times(x, cosine, sine):
    return x[0] * cosine - x[1] * sine, x[0] * sine + x[1] * cosine


def plus(x, y):
    return x[0] + y[0], x[1] + y[1]


def minus(x, y):
    return x[0] - y[0], x[1] - y[1]


def quarter(x, sign):
    return (-x[1], x[0]) if sign > 0 else (x[1], -x[0])


def turned(x, eighths, sign):
    eighths %= 16
    if eighths == 0:
        return x
    if eighths == 4:
        return quarter(x, sign)
    if eighths == 2 or eighths == 6:
        root = math.sqrt(0.5)
        real, imaginary = x if eighths == 2 else quarter(x, sign)
        if sign > 0:
            return (real - imaginary) * root, (real + imaginary) * root
        return (real + imaginary) * root, (imaginary - real) * root
    angle = sign * 2.0 * math.pi * eighths / 16
    return times(x, math.cos(angle), math.sin(angle))


def four(x, sign):
    a, b = plus(x[0], x[2]), minus(x[0], x[2])
    c, d = plus(x[1], x[3]), quarter(minus(x[1], x[3]), sign)
    return [plus(a, c), plus(b, d), minus(a, c), minus(b, d)]


def sixteen(x, sign):
    inner = [four([x[4 * p + q] for p in range(4)], sign) for q in range(4)]
    out = [None] * 16
    for a in range(4):
        outer = four([turned(inner[q][a], q * a, sign) for q in range(4)], sign)
        for b in range(4):
            out[a + 4 * b] = outer[b]
    return out


def eight(x, sign):
    even, odd = four(x[0::2], sign), four(x[1::2], sign)
    odd = [turned(odd[i], 2 * i, sign) for i in range(4)]
    return [plus(even[i], odd[i]) for i in range(4)] + [minus(even[i], odd[i]) for i in range(4)]


def forward_kernel(k_ref, first_ref, twist_ref, second_ref, o_ref, l_ref):
    for r in range(8):
        row = k_ref[r]
        a = dot(first_ref[...], jnp.concatenate([row, row], axis=0))
        real, imaginary = times((a[:HELD], a[HELD:]), twist_ref[0], twist_ref[1])
        high, low = split(jnp.concatenate([real, imaginary], axis=1))
        l_ref[pl.ds(r * HELD, HELD), :] = jnp.concatenate([high, low, high], axis=1)
    out = dot(l_ref[...], second_ref[...])
    for part in range(2):
        piece = out[:, 128 * part : 128 * part + 128].reshape(8, HELD, 128)
        o_ref[:, part] = jnp.swapaxes(piece, 0, 1)


def whole(shape):
    return pl.BlockSpec(shape, lambda *_: (0,) * len(shape), pipeline_mode=pl.Buffered(1))


def forward(rows):
    first, twist, second = (jnp.asarray(x) for x in forward_tables())
    return pl.pallas_call(
        forward_kernel,
        grid=(16,),
        in_specs=[
            pl.BlockSpec((8, None, 64, 256), lambda v: (0, v, 0, 0)),
            whole(first.shape),
            whole(twist.shape),
            whole(second.shape),
        ],
        out_specs=pl.BlockSpec((HELD, 2, 8, 128), lambda v: (0, 0, v, 0)),
        out_shape=jax.ShapeDtypeStruct((HELD, 2, 128, 128), jnp.float32),
        scratch_shapes=[pltpu.VMEM((8 * HELD, 1536), jnp.bfloat16)],
        compiler_params=pltpu.CompilerParams(vmem_limit_bytes=62 << 20),
        cost_estimate=pl.CostEstimate(flops=2 * 128 * HELD * 2500 * 256, bytes_accessed=8 << 20, transcendentals=0),
        name="forward",
    )(rows, first, twist, second)


def filter_rows(z_ref, position, x_ref_twist, waves_ref, squares_ref, s_ref, q_ref):
    group, j = position // 8, position % 8
    for part in range(2):
        rows = pl.ds(pl.multiple_of(group * 16 + part * 8, 8), 8)
        square = squares_ref[rows, :]
        values = []
        for v in range(16):
            x = z_ref[v * 16 + part * 8 : v * 16 + part * 8 + 8, :128], z_ref[v * 16 + part * 8 : v * 16 + part * 8 + 8, 128:]
            if v:
                x = times(x, x_ref_twist[j, 2 * v : 2 * v + 1, :], x_ref_twist[j, 2 * v + 1 : 2 * v + 2, :])
            values.append(x)
        values = sixteen(values, -1)
        q_ref[j, 0, rows, :] = values[8][0] + jnp.where(square == 0.0, values[0][0], 0.0)
        q_ref[j, 1, rows, :] = values[8][1] + jnp.where(square == 0.0, values[0][1], 0.0)
        totals = None
        for a in range(16):
            wave = waves_ref[j, a : a + 1, :]
            below = waves_ref[j, 16 + a : 17 + a, :] + square
            if a == 0:
                scale = jnp.where(below > 0.0, 1.0 / jnp.where(below > 0.0, below, 1.0), 0.0)
            else:
                scale = 1.0 / below
            if a == 8:
                scale = scale * waves_ref[j, 32:33, :]
            real, imaginary = values[a][0] * scale, values[a][1] * scale
            terms = [real, imaginary, real * wave, imaginary * wave]
            totals = terms if totals is None else [p + t for p, t in zip(totals, terms)]
        for f in range(4):
            s_ref[f, j, rows, :] = totals[f]


def row_chunk(x_ref, squares_ref, grid_ref, twist_ref, waves_ref, back_ref, left_ref, o_ref, l_ref, z0_ref, z1_ref, s_ref, q_ref, g_ref, r_ref, line_ref, between):
    def arrange(v, _):
        rows = pl.ds(pl.multiple_of(v * 8, 8), 8)
        real = x_ref[:, 0, rows, :].reshape(128, 128)
        imaginary = x_ref[:, 1, rows, :].reshape(128, 128)
        high, low = split(jnp.concatenate([real.T, imaginary.T], axis=1))
        l_ref[:, v] = jnp.concatenate([high, low, high], axis=1).reshape(8, 16, 768)
        return 0

    lax.fori_loop(0, 16, arrange, 0)

    def multiply(position, z_ref):
        z_ref[...] = dot(l_ref[position // 8].reshape(256, 768), grid_ref[position % 8])

    def filtered(position, z_ref):
        filter_rows(z_ref, position, twist_ref, waves_ref, squares_ref, s_ref, q_ref)

    multiply(0, z0_ref)

    def pair(h, _):
        multiply(2 * h + 1, z1_ref)
        filtered(2 * h, z0_ref)
        multiply(jnp.minimum(2 * h + 2, 63), z0_ref)
        filtered(2 * h + 1, z1_ref)
        return 0

    def segment(g, _):
        lax.fori_loop(0, 4, lambda h, c: pair(4 * g + h, c), 0)
        between(g)
        return 0

    lax.fori_loop(0, 7, segment, 0)
    lax.fori_loop(28, 32, pair, 0)

    def unfold(group, _):
        rows = pl.ds(pl.multiple_of(group * 16, 16), 16)
        for f in range(2):
            values = eight([(s_ref[2 * f, j, rows, :], s_ref[2 * f + 1, j, rows, :]) for j in range(8)], 1)
            for i in range(8):
                real, imaginary = times(values[i], back_ref[2 * i : 2 * i + 1, :], back_ref[2 * i + 1 : 2 * i + 2, :])
                high, low = split(jnp.concatenate([real, imaginary], axis=1))
                g_ref[8 * f + i, rows, :] = jnp.concatenate([high, low, high], axis=1)
        return 0

    lax.fori_loop(0, 8, unfold, 0)

    def outward(q, _):
        for e in range(4):
            result = lax.dot_general(left_ref[...], g_ref[4 * q + e], (((1,), (1,)), ((), ())), preferred_element_type=jnp.float32)
            r_ref[2 * e] = result[:128]
            r_ref[2 * e + 1] = result[128:]
        o_ref[:, pl.ds(pl.multiple_of(q * 8, 8), 8), :] = jnp.swapaxes(r_ref[...], 0, 1)
        return 0

    lax.fori_loop(0, 4, outward, 0)
    lines = jnp.zeros((8, 128), jnp.float32)
    for part in range(2):
        line = q_ref[0, part].T[0:1] * (1.0 / N / N)
        place = lax.broadcasted_iota(jnp.int32, (8, 128), 0) == part
        lines = lines + jnp.where(place, jnp.broadcast_to(line, (8, 128)), 0.0)
    line_ref[...] = lines


def exchange_kernel(
    sent_ref, squares_ref, grid_ref, twist_ref, waves_ref, back_ref, left_ref, o_ref,
    arrived_ref, partial_ref, lines_ref, slot_ref, turn_ref, reduced_ref, landed_ref, l_ref, z0_ref, z1_ref, s_ref, q_ref, g_ref, r_ref,
    own_sem, in_send, in_recv, ring_send, ring_recv, turn_send, turn_recv, back_send, back_recv,
):
    y, z = lax.axis_index("col"), lax.axis_index("row")
    right, left = lax.rem(z + 1, DEEP), lax.rem(z + DEEP - 1, DEEP)
    barrier = pltpu.get_barrier_semaphore()

    def greet(d, _):
        pl.semaphore_signal(barrier, inc=1, device_id={"col": lax.rem(y + d, COLS)}, device_id_type=pl.DeviceIdType.MESH)
        return 0

    lax.fori_loop(1, COLS, greet, 0)
    for neighbour in (left, right):
        pl.semaphore_signal(barrier, inc=1, device_id={"row": neighbour}, device_id_type=pl.DeviceIdType.MESH)
    pl.semaphore_wait(barrier, COLS + 1)

    def inward(k, d):
        peer = lax.rem(y + d, COLS)
        return pltpu.make_async_remote_copy(
            sent_ref.at[k, peer], arrived_ref.at[k, y], in_send.at[k, d], in_recv.at[k, d],
            device_id={"col": peer}, device_id_type=pl.DeviceIdType.MESH,
        )

    def own(k):
        return pltpu.make_async_copy(sent_ref.at[k, y], arrived_ref.at[k, y], own_sem.at[k])

    def homeward(k, d):
        peer = lax.rem(y + d, COLS)
        rows = pl.ds(pl.multiple_of(k * ROWS, 8), ROWS)
        return pltpu.make_async_remote_copy(
            reduced_ref.at[k, peer], landed_ref.at[y, rows], back_send.at[k, d], back_recv.at[k, d],
            device_id={"col": peer}, device_id_type=pl.DeviceIdType.MESH,
        )

    def share(block, lane):
        return pl.ds(lax.rem(block + 2 * DEEP, DEEP) * COLS + 2 * lane, 2)

    def ring(k, lane, s, source):
        return pltpu.make_async_remote_copy(
            source, slot_ref.at[k, lane, s], ring_send.at[k, lane, s], ring_recv.at[k, lane, s],
            device_id={"row": right if lane % 2 == 0 else left}, device_id_type=pl.DeviceIdType.MESH,
        )

    def turn(k, s, source):
        return pltpu.make_async_remote_copy(
            source, turn_ref.at[k, s], turn_send.at[k, s], turn_recv.at[k, s],
            device_id={"row": right}, device_id_type=pl.DeviceIdType.MESH,
        )

    def open_ring(k):
        turn(k, 0, lines_ref.at[k]).start()
        for lane in range(LANES):
            block = z - 1 if lane % 2 == 0 else z + 1
            ring(k, lane, 0, partial_ref.at[k, share(block, lane)]).start()

    def step(k, s):
        turn(k, s, turn_ref.at[k, s]).wait_recv()
        lines = turn_ref[k, s] + lines_ref[k]

        @pl.when(s < DEEP - 2)
        def _():
            turn_ref[k, s] = lines
            turn(k, s + 1, turn_ref.at[k, s]).start()

        @pl.when(s == DEEP - 2)
        def _():
            reduced_ref[k, :, 32:40] = jnp.broadcast_to(lines[None], (COLS, 8, 128))

        for lane in range(LANES):
            ring(k, lane, s, slot_ref.at[k, lane, s]).wait_recv()
            block = z - s - 2 if lane % 2 == 0 else z + s + 2
            total = slot_ref[k, lane, s] + partial_ref[k, share(block, lane)]

            @pl.when(s < DEEP - 2)
            def _():
                slot_ref[k, lane, s] = total
                ring(k, lane, s + 1, slot_ref.at[k, lane, s]).start()

            @pl.when(s == DEEP - 2)
            def _():
                reduced_ref[k, 2 * lane : 2 * lane + 2, 0:32] = total

    def close_ring(k):
        landed_ref[y, pl.ds(pl.multiple_of(k * ROWS, 8), ROWS), :] = reduced_ref[k, y]

        def give(d, _):
            homeward(k, d).start()
            return 0

        lax.fori_loop(1, COLS, give, 0)

    def launch(k, _):
        own(k).start()

        def give(d, _):
            inward(k, d).start()
            return 0

        lax.fori_loop(1, COLS, give, 0)
        return 0

    launch(0, 0)

    def chunk(k, _):
        own(k).wait()

        def take(d, _):
            inward(k, d).wait_recv()
            return 0

        lax.fori_loop(1, COLS, take, 0)

        @pl.when(k == 0)
        def _():
            launch(1, 0)

        @pl.when(k > 0)
        def _():
            open_ring(k - 1)

        def between(g):
            @pl.when((k > 0) & (g % 2 == 0))
            def _():
                step(k - 1, g // 2)

            @pl.when((k > 1) & (g % 2 == 1))
            def _():
                step(k - 2, 4 + g // 2)

            @pl.when((k < CHUNKS - 2) & (g == 5))
            def _():
                launch(k + 2, 0)

        row_chunk(
            arrived_ref.at[k], squares_ref.at[k], grid_ref, twist_ref, waves_ref, back_ref, left_ref,
            partial_ref.at[k], l_ref, z0_ref, z1_ref, s_ref, q_ref, g_ref, r_ref, lines_ref.at[k], between,
        )

        @pl.when(k > 1)
        def _():
            close_ring(k - 2)

        return 0

    lax.fori_loop(0, CHUNKS, chunk, 0)
    open_ring(CHUNKS - 1)

    def both(s, _):
        step(CHUNKS - 2, 4 + s)
        step(CHUNKS - 1, s)
        return 0

    def last(s, _):
        step(CHUNKS - 1, s)
        return 0

    lax.fori_loop(0, 3, both, 0)
    close_ring(CHUNKS - 2)
    lax.fori_loop(3, DEEP - 1, last, 0)
    close_ring(CHUNKS - 1)

    def settle(k, _):
        def one(d, _):
            inward(k, d).wait_send()
            homeward(k, d).wait_send()
            homeward(k, d).wait_recv()
            return 0

        lax.fori_loop(1, COLS, one, 0)

        def two(s, _):
            turn(k, s, turn_ref.at[k, s]).wait_send()
            for lane in range(LANES):
                ring(k, lane, s, slot_ref.at[k, lane, s]).wait_send()
            return 0

        lax.fori_loop(0, DEEP - 1, two, 0)
        return 0

    lax.fori_loop(0, CHUNKS, settle, 0)
    o_ref[...] = landed_ref[...]


def exchange(sent, y, z):
    tables = [jnp.asarray(x) for x in row_tables()]
    tables[3] = lax.dynamic_index_in_dim(tables[3], z, 0, keepdims=False)
    t = 4 * y + jnp.arange(CHUNKS, dtype=jnp.int32)
    wave = STEP * (64 * jnp.arange(128, dtype=jnp.int32)[None, :] + t[:, None]).astype(jnp.float32)
    squares = jnp.broadcast_to((wave * wave)[:, :, None], (CHUNKS, 128, 128))
    vmem = pl.BlockSpec(memory_space=pltpu.VMEM)
    return pl.pallas_call(
        exchange_kernel,
        in_specs=[pl.BlockSpec(memory_space=pl.ANY)] + [vmem] * (1 + len(tables)),
        out_specs=vmem,
        out_shape=jax.ShapeDtypeStruct((COLS, CHUNKS * ROWS, 128), jnp.float32),
        scratch_shapes=[
            pltpu.VMEM((CHUNKS, COLS, 2, 128, 128), jnp.float32),
            pltpu.VMEM((CHUNKS, 128, 32, 128), jnp.float32),
            pltpu.VMEM((CHUNKS, 8, 128), jnp.float32),
            pltpu.VMEM((CHUNKS, LANES, DEEP - 1, 2, 32, 128), jnp.float32),
            pltpu.VMEM((CHUNKS, DEEP - 1, 8, 128), jnp.float32),
            pltpu.VMEM((CHUNKS, COLS, ROWS, 128), jnp.float32),
            pltpu.VMEM((COLS, CHUNKS * ROWS, 128), jnp.float32),
            pltpu.VMEM((8, 16, 16, 768), jnp.bfloat16),
            pltpu.VMEM((256, 256), jnp.float32),
            pltpu.VMEM((256, 256), jnp.float32),
            pltpu.VMEM((4, 8, 128, 128), jnp.float32),
            pltpu.VMEM((8, 2, 128, 128), jnp.float32),
            pltpu.VMEM((16, 128, 768), jnp.bfloat16),
            pltpu.VMEM((8, 128, 128), jnp.float32),
            pltpu.SemaphoreType.DMA((CHUNKS,)),
            pltpu.SemaphoreType.DMA((CHUNKS, COLS)),
            pltpu.SemaphoreType.DMA((CHUNKS, COLS)),
            pltpu.SemaphoreType.DMA((CHUNKS, LANES, DEEP - 1)),
            pltpu.SemaphoreType.DMA((CHUNKS, LANES, DEEP - 1)),
            pltpu.SemaphoreType.DMA((CHUNKS, DEEP - 1)),
            pltpu.SemaphoreType.DMA((CHUNKS, DEEP - 1)),
            pltpu.SemaphoreType.DMA((CHUNKS, COLS)),
            pltpu.SemaphoreType.DMA((CHUNKS, COLS)),
        ],
        compiler_params=pltpu.CompilerParams(vmem_limit_bytes=63 << 20, collective_id=0, has_side_effects=True),
        name="exchange",
    )(sent.reshape(CHUNKS, COLS, 2, 128, 128), squares, *tables)


def final_kernel(*refs):
    y_ref, w_ref, state_hbm, rows_hbm, first_ref, twist_ref, second_ref, scales_ref, o_ref, a_ref, r_ref, f_ref, held_ref, send_sem, recv_sem, load_sem, k_ref, kept_sem = refs
    kept = pltpu.make_async_copy(rows_hbm.at[:, 0], k_ref, kept_sem)
    kept.start()
    shell = lax.axis_index("shell")
    barrier = pltpu.get_barrier_semaphore()
    pl.semaphore_signal(barrier, inc=1, device_id={"shell": 1 - shell}, device_id_type=pl.DeviceIdType.MESH)
    pl.semaphore_wait(barrier, 1)
    loaded = pltpu.make_async_copy(state_hbm, held_ref, load_sem)

    @pl.when(shell == 0)
    def _():
        loaded.start()

    for k in range(CHUNKS):
        for q in range(5):
            block = jnp.swapaxes(y_ref[:, ROWS * k + 8 * q : ROWS * k + 8 * q + 8, :], 0, 1)
            a_ref[8 * q : 8 * q + 8, 16 * k : 16 * k + 16, :] = block

    def synthesis(pairs):
        high, low = split(jnp.concatenate([jnp.concatenate(p, axis=1) for p in pairs], axis=0))
        out = dot(jnp.concatenate([high, low, high], axis=1), first_ref[...])
        results = []
        for f in range(len(pairs)):
            x = out[64 * f : 64 * f + 64, :256], out[64 * f : 64 * f + 64, 256:]
            high, low = split(jnp.concatenate(times(x, twist_ref[0], twist_ref[1]), axis=0))
            results.append(dot(second_ref[...], jnp.concatenate([high, low, high], axis=0)))
        return results

    weight = scales_ref[0]
    r_ref[...] = synthesis([(a_ref[32] * weight, a_ref[33] * weight)])[0]
    sign = (1 - 2 * (lax.broadcasted_iota(jnp.int32, (64, 256), 1) % 2)).astype(jnp.float32)

    def ray(i, _):
        base = a_ref[2 * i], a_ref[2 * i + 1]
        slope = a_ref[16 + 2 * i], a_ref[17 + 2 * i]
        one, wave, square = scales_ref[0], scales_ref[1], scales_ref[2]
        alpha_rows, alpha_cols, curve_cols, curve_mixed = synthesis(
            [
                (-slope[1] * one, slope[0] * one),
                (-base[1] * wave, base[0] * wave),
                (-base[0] * square, -base[1] * square),
                (-slope[0] * wave, -slope[1] * wave),
            ]
        )
        kappa = k_ref[i].astype(jnp.float32)
        edge = sign * (jnp.sum(kappa * sign) * (1.0 / N))
        curve_rows = 2.0 * (kappa - edge - r_ref[...]) - curve_cols
        for f, field in enumerate([alpha_rows, alpha_cols, curve_rows, curve_cols, curve_mixed]):
            f_ref[f, i] = field
        return 0

    kept.wait()
    lax.fori_loop(0, 8, ray, 0)

    def passed(g):
        part = (slice(None), slice(None), pl.ds(pl.multiple_of(2048 * g, 2048), 2048))
        return pltpu.make_async_remote_copy(
            o_ref.at[part], held_ref.at[part], send_sem.at[g], recv_sem.at[g],
            device_id={"shell": 1 - shell}, device_id_type=pl.DeviceIdType.MESH,
        )

    def emit(g, source_ref):
        blocks = [jnp.swapaxes(f_ref[f, :, pl.ds(pl.multiple_of(8 * g, 8), 8), :], 0, 1) for f in range(5)]
        for v in range(8):
            place = pl.ds(pl.multiple_of((8 * g + v) * 256, 256), 256)
            fields = [block[v] for block in blocks]
            for e, value in enumerate(moved([source_ref[e, :, place] for e in range(6)], fields, w_ref[0])):
                o_ref[e, :, place] = value

    def opening(g, _):
        emit(g, held_ref)
        passed(g).start()
        return 0

    def closing(g, _):
        passed(g).wait_recv()
        emit(g, held_ref)
        return 0

    def settled(g, _):
        passed(g).wait_send()
        return 0

    @pl.when(shell == 0)
    def _():
        loaded.wait()
        lax.fori_loop(0, 8, opening, 0)
        lax.fori_loop(0, 8, settled, 0)

    @pl.when(shell == 1)
    def _():
        lax.fori_loop(0, 8, closing, 0)


def moved(state, fields, w):
    rows, cols, mixed = w * fields[2], w * fields[3], w * fields[4]
    upper_left, upper_right, lower_left, lower_right = state[2:]
    return [
        state[0] - w * fields[0],
        state[1] - w * fields[1],
        upper_left - (rows * upper_left + mixed * lower_left),
        upper_right - (rows * upper_right + mixed * lower_right),
        lower_left - (mixed * upper_left + cols * lower_left),
        lower_right - (mixed * upper_right + cols * lower_right),
    ]


def final_stage(returned, rows, weight, state):
    tables = [jnp.asarray(x) for x in final_tables()]
    vmem = pl.BlockSpec(memory_space=pltpu.VMEM)
    return pl.pallas_call(
        final_kernel,
        in_specs=[vmem, pl.BlockSpec(memory_space=pltpu.SMEM), pl.BlockSpec(memory_space=pl.ANY), pl.BlockSpec(memory_space=pl.ANY)]
        + [vmem] * len(tables),
        out_specs=vmem,
        out_shape=jax.ShapeDtypeStruct((6, 8, N), jnp.float32),
        scratch_shapes=[
            pltpu.VMEM((40, 64, 128), jnp.float32),
            pltpu.VMEM((64, 256), jnp.float32),
            pltpu.VMEM((5, 8, 64, 256), jnp.float32),
            pltpu.VMEM((6, 8, N), jnp.float32),
            pltpu.SemaphoreType.DMA((8,)),
            pltpu.SemaphoreType.DMA((8,)),
            pltpu.SemaphoreType.DMA,
            pltpu.VMEM((8, 64, 256), jnp.bfloat16),
            pltpu.SemaphoreType.DMA,
        ],
        compiler_params=pltpu.CompilerParams(vmem_limit_bytes=62 << 20, collective_id=1, has_side_effects=True),
        name="final_stage",
    )(returned, weight, state, rows, *tables)


def body(convergence, lens_weight, rays_in):
    y, z = lax.axis_index("col"), lax.axis_index("row")
    rows = convergence.reshape(8, 16, 64, 256)
    returned = exchange(forward(rows), y, z)
    return final_stage(returned, rows, lens_weight, rays_in)[None]


def solution(mesh):
    in_specs = (P("shell", ("row", "col"), None), P("shell"), P(None, ("row", "col"), None))
    out_specs = P("shell", None, ("row", "col"), None)
    return jax.shard_map(body, mesh=mesh, in_specs=in_specs, out_specs=out_specs, check_vma=False)
```
